768 devices in a mesh: gx: 16 (over z_hi, x, core), gy: 48 (over y, z_lo).
Axes of the slice: x: 4, y: 8, z: 12 (z_hi: 2, z_lo: 6; z = z_hi * 6 + z_lo), core: 2. Of those that a mesh axis runs over, the one named last changes fastest.
Arguments:
- adj_electric: float32 [3, 512, 384, 128], P(None, 'gx', 'gy'), may hold values from -6 to 6
- adj_magnetic: float32 [3, 512, 384, 128], P(None, 'gx', 'gy'), may hold values from -6 to 6
- polarization: float32 [3, 512, 384, 128], P(None, 'gx', 'gy'), may hold values from -6 to 6
- pol_rate: float32 [3, 512, 384, 128], P(None, 'gx', 'gy'), may hold values from -6 to 6
- density: float32 [512, 384, 128], P('gx', 'gy'), may hold values from 0 to 1
- forward_rate: float32 [2, 3, 512, 384, 128], P(None, None, 'gx', 'gy'), may hold values from -6 to 6
- design_mask: int32 [512, 384, 128], P('gx', 'gy'), may hold values 0 or 1
- partner_rows: int32 [384], P('gy'), may hold values from 0 to 7, as said below
- filter_radius: int32 [512, 384], P('gx', 'gy'), may hold values from 1 to 4
Outputs:
- electric_out: float32 [3, 512, 384, 128], P(None, 'gx', 'gy')
- magnetic_out: float32 [3, 512, 384, 128], P(None, 'gx', 'gy')
- density_out: float32 [512, 384, 128], P('gx', 'gy')
The draws below stay inside these ranges and needn't reach their ends.
Inputs may be any that keep to these rules, and one draw needn't show every extreme that they name: `partner_rows`: within each block of 8 rows the values are a permutation of 0 to 7.
All inputs are finite; a program needn't handle non-finite values. No bound on the sum of `design_mask` on one device may be relied on, other than what follows from the above.
Results may differ from the reference program's by a relative error of at most 0.0001.
Values sent between devices are 32-bit elements; how exact they have to be, the bound alone decides.
A program may use at most 32 MiB of HBM per device.

```python
import math
import jax
import jax.numpy as jnp
from jax import lax

CY = 8
STEPS = 2
RMAX = 4
NX = 512
NY = 384
NZ = 128


def draw_partner_rows(key, part):
    blocks = NY // CY
    keys = jax.random.split(jax.random.fold_in(key, 11), blocks)
    perms = jax.vmap(lambda single: jax.random.permutation(single, CY))(keys)
    return perms.reshape(NY).astype(jnp.int32)


def draw_filter_radius(key, part):
    first, second, third = jax.random.split(jax.random.fold_in(key, 23), 3)
    radius = jax.random.randint(first, (NX, NY), 1, RMAX + 1)
    where_x = jax.random.randint(second, (), 0, NX)
    where_y = jax.random.randint(third, (), 0, NY)
    return radius.at[where_x, where_y].set(RMAX).astype(jnp.int32)


def plant(result, key, low, largest):
    longest = result.shape.index(max(result.shape))
    spots = []
    for shift in (0, 1):
        where = [jax.random.randint(jax.random.fold_in(key, axis), (), 0, length) for axis, length in enumerate(result.shape)]
        where[longest] = (where[longest] + shift) % result.shape[longest]
        spots.append(tuple(where))
    return result.at[spots[0]].set(low).at[spots[1]].set(largest)


def shard_levels(rng, extent, cuts, least, high):
    factor_of = 1.0
    for position, parts in cuts:
        draws = jax.random.uniform(jax.random.fold_in(jax.random.fold_in(rng, 6), position), (parts,), jnp.float32, least / len(cuts), high / len(cuts))
        factor_of = factor_of * jnp.repeat(jnp.exp(draws), extent[position] // parts).reshape((-1,) + (1,) * (len(extent) - 1 - position))
    return factor_of


def noise(stream_key, shape, scale, bound, pieces=(), kind=jnp.bfloat16):
    level = shard_levels(stream_key, shape, pieces, -0.22, 0.18) if pieces else 1.0
    entries = jax.random.normal(stream_key, shape, jnp.float32) * scale * level
    return jnp.minimum(jnp.maximum(entries, -bound), bound).astype(kind)


def setup_inputs(seed: int = 0) -> dict:
    streams_of = jax.random.split(jax.random.key(seed), 10)
    adj_electric = noise(streams_of[0], (3, NX, NY, NZ), 1.0, 6.0, ((1, 16), (2, 48)), jnp.float32)
    adj_magnetic = noise(streams_of[1], (3, NX, NY, NZ), 1.0, 6.0, ((1, 16), (2, 48)), jnp.float32)
    polarization = noise(streams_of[2], (3, NX, NY, NZ), 1.0, 6.0, ((1, 16), (2, 48)), jnp.float32)
    pol_rate = noise(streams_of[3], (3, NX, NY, NZ), 1.0, 6.0, ((1, 16), (2, 48)), jnp.float32)
    density = jnp.clip(1.0 * jax.random.uniform(streams_of[4], (NX, NY, NZ), jnp.float32) ** shard_levels(streams_of[4], (NX, NY, NZ), ((0, 16), (1, 48)), -0.2, 0.2), 0.0, 1.0)
    forward_rate = noise(streams_of[5], (STEPS, 3, NX, NY, NZ), 1.0, 6.0, ((2, 16), (3, 48)), jnp.float32)
    design_mask = plant((jax.random.randint(streams_of[6], (NX, NY, NZ), 0, 4) < 3).astype(jnp.int32), jax.random.fold_in(streams_of[6], 1), 0, 1)
    partner_rows = draw_partner_rows(jax.random.fold_in(streams_of[9], 71), 0)
    filter_radius = draw_filter_radius(jax.random.fold_in(streams_of[9], 71), 0)
    return dict(adj_electric=adj_electric, adj_magnetic=adj_magnetic, polarization=polarization, pol_rate=pol_rate, density=density, forward_rate=forward_rate, design_mask=design_mask, partner_rows=partner_rows, filter_radius=filter_radius)


COURANT = 0.5
DAMPING = 0.9
OMEGA_SQUARED = 0.3
LORENTZ_STRENGTH = 2.0
EPS_MATERIAL = 4.0
UPDATE_STEP = 0.25
SHARPNESS = 4.0
THRESHOLD = 0.5

def ahead(values, dimension):
    count = values.shape[dimension]
    rest = lax.slice_in_dim(values, 1, count, axis=dimension)
    edge = jnp.zeros_like(lax.slice_in_dim(values, 0, 1, axis=dimension))
    return jnp.concatenate([rest, edge], dimension)

def behind(values, dimension):
    count = values.shape[dimension]
    rest = lax.slice_in_dim(values, 0, count - 1, axis=dimension)
    edge = jnp.zeros_like(lax.slice_in_dim(values, 0, 1, axis=dimension))
    return jnp.concatenate([edge, rest], dimension)

def advance(electric, magnetic, polar_now, velocity, material, inside):
    eps_local = 1.0 + (EPS_MATERIAL - 1.0) * material
    e_x, e_y, e_z = (electric[0], electric[1], electric[2])
    curl_e = jnp.stack([ahead(e_z, 1) - e_z - (ahead(e_y, 2) - e_y), ahead(e_x, 2) - e_x - (ahead(e_z, 0) - e_z), ahead(e_y, 0) - e_y - (ahead(e_x, 1) - e_x)])
    magnetic = (magnetic - COURANT * curl_e) * inside
    h_x, h_y, h_z = (magnetic[0], magnetic[1], magnetic[2])
    curl_h = jnp.stack([h_z - behind(h_z, 1) - (h_y - behind(h_y, 2)), h_x - behind(h_x, 2) - (h_z - behind(h_z, 0)), h_y - behind(h_y, 0) - (h_x - behind(h_x, 1))])
    velocity = DAMPING * velocity - OMEGA_SQUARED * polar_now + OMEGA_SQUARED * LORENTZ_STRENGTH * material * electric
    polar_now = polar_now + velocity
    electric = (electric + (COURANT * curl_h - velocity) / eps_local) * inside
    return (electric, magnetic, polar_now, velocity)

def project(filtered):
    top = math.tanh(SHARPNESS * THRESHOLD)
    bottom = top + math.tanh(SHARPNESS * (1.0 - THRESHOLD))
    return (top + jnp.tanh(SHARPNESS * (filtered - THRESHOLD))) / bottom

def reference(adj_electric, adj_magnetic, polarization, pol_rate, density, forward_rate, design_mask, partner_rows, filter_radius):
    electric, magnetic, polar_now, velocity = (adj_electric, adj_magnetic, polarization, pol_rate)
    gradient = jnp.zeros(density.shape, jnp.float32)
    for step_index in range(STEPS):
        electric, magnetic, polar_now, velocity = advance(electric, magnetic, polar_now, velocity, density, 1.0)
        gradient = gradient + lax.optimization_barrier(jnp.sum(electric * forward_rate[step_index], axis=0))
    row_index = jnp.arange(NY, dtype=jnp.int32) // CY * CY + partner_rows.astype(jnp.int32)
    mirrored = jnp.take(gradient[::-1], row_index, axis=1)
    symmetric = 0.5 * (gradient + mirrored)
    updated = density - UPDATE_STEP * design_mask.astype(jnp.float32) * symmetric
    width = RMAX - 1
    framed = jnp.pad(updated, ((width, width), (width, width), (0, 0)))
    covered = jnp.pad(jnp.ones((NX, NY, 1), jnp.float32), ((width, width), (width, width), (0, 0)))
    radius = filter_radius.astype(jnp.float32)[:, :, None]
    numer = jnp.zeros(density.shape, jnp.float32)
    denom = jnp.zeros((NX, NY, 1), jnp.float32)
    for shift_x in range(-width, width + 1):
        for shift_y in range(-width, width + 1):
            distance = math.sqrt(shift_x * shift_x + shift_y * shift_y)
            weight = jnp.maximum(radius - distance, 0.0)
            window = framed[width + shift_x:width + shift_x + NX, width + shift_y:width + shift_y + NY, :]
            inside = covered[width + shift_x:width + shift_x + NX, width + shift_y:width + shift_y + NY, :]
            numer = numer + weight * (inside * window)
            denom = denom + weight * inside
    density_out = project(numer / denom)
    return (electric, magnetic, density_out)
```

```python
import functools
import math

import jax
import jax.numpy as jnp
from jax import lax
from jax.experimental import pallas as pl
from jax.experimental.pallas import tpu as pltpu
from jax.sharding import PartitionSpec as P

STEPS = 2
RMAX = 4
COURANT = 0.5
DAMPING = 0.9
OMEGA_SQUARED = 0.3
LORENTZ_STRENGTH = 2.0
EPS_MATERIAL = 4.0
UPDATE_STEP = 0.25
SHARPNESS = 4.0
THRESHOLD = 0.5

MESH = pl.DeviceIdType.MESH
WIDTH = RMAX - 1
EDGE = 8
ORDER = (0, 2, 1)
SIDES = tuple((i, j) for i in (-1, 0, 1) for j in (-1, 0, 1) if (i, j) != (0, 0))


def kernel(
    nx,
    ny,
    electric_in,
    magnetic_in,
    polar_in,
    rate_in,
    density_in,
    forward_in,
    mask_in,
    partner_in,
    radius_in,
    electric_out,
    magnetic_out,
    density_out,
    v_electric,
    v_magnetic,
    v_polar,
    v_rate,
    v_density,
    v_forward,
    v_mask,
    v_radius,
    efield,
    hfield,
    polar,
    rate,
    inv_eps,
    gradient,
    g_send,
    g_recv,
    g_flip,
    updated,
    covered,
    sums,
    weight_radius,
    inv_denom,
    ye_recv,
    yh_send,
    yh_recv,
    xe_send,
    xe_recv,
    xh_send,
    xh_recv,
    d1_recv,
    d2_recv,
    xf_send,
    xf_recv,
    yf_send,
    yf_recv,
    cf_recv,
    o_electric,
    o_magnetic,
    o_density,
    in_sems,
    out_sems,
    send_sems,
    recv_sems,
):
    rows_x, rows_y = v_radius.shape
    slab = rows_x + 2 * EDGE

    def rows(y, first=EDGE, count=rows_x):
        return pl.ds(y * slab + first, count)

    def own(y):
        start = y * slab + EDGE
        return pl.ds(start if isinstance(start, int) else pl.multiple_of(start, EDGE), rows_x)

    def edge(y, first):
        start = y * slab + first
        return pl.ds(start if isinstance(start, int) else pl.multiple_of(start, EDGE), EDGE)

    gx, gy = lax.axis_index("gx"), lax.axis_index("gy")
    has = {}
    for i, j in SIDES:
        parts = []
        if i:
            parts.append(gx > 0 if i < 0 else gx < nx - 1)
        if j:
            parts.append(gy > 0 if j < 0 else gy < ny - 1)
        has[i, j] = functools.reduce(jnp.logical_and, parts)

    def device(i, j):
        return (lax.rem(gx + i + nx, nx), lax.rem(gy + j + ny, ny))

    mirror = (nx - 1 - gx, gy)

    loads = [
        pltpu.make_async_copy(src, dst, in_sems.at[k])
        for k, (src, dst) in enumerate(
            [
                (electric_in, v_electric),
                (magnetic_in, v_magnetic),
                (polar_in, v_polar),
                (rate_in, v_rate),
                (density_in, v_density),
                (forward_in, v_forward),
                (mask_in, v_mask),
                (radius_in, v_radius),
            ]
        )
    ]
    for load in loads:
        load.start()

    barrier = pltpu.get_barrier_semaphore()
    greeted = jnp.int32(1)
    for side in SIDES:
        greeted = greeted + has[side].astype(jnp.int32)

        @pl.when(has[side])
        def _():
            pl.semaphore_signal(barrier, inc=1, device_id=device(*side), device_id_type=MESH)

    pl.semaphore_signal(barrier, inc=1, device_id=mirror, device_id_type=MESH)

    lane = lax.broadcasted_iota(jnp.int32, (rows_x, 128), 1)

    def ahead_z(v):
        return jnp.where(lane < 127, pltpu.roll(v, 127, 1), 0.0)

    def behind_z(v):
        return jnp.where(lane > 0, pltpu.roll(v, 1, 1), 0.0)

    def over_rows(body, count=rows_y):
        def step(y, carry):
            body(y)
            return carry

        lax.fori_loop(0, count, step, 0)

    zeros_slab = jnp.zeros((rows_x, 128), jnp.float32)
    zeros_edge = jnp.zeros((EDGE, 128), jnp.float32)
    for s in range(STEPS):
        for c in range(3):
            efield[s, c, own(rows_y), :] = zeros_slab

            def clear(y, s=s, c=c):
                efield[s, c, edge(y, EDGE + rows_x), :] = zeros_edge

            over_rows(clear)

    for s in range(STEPS):
        for refs, shape, side in (
            (ye_recv, zeros_slab, (0, 1)),
            (yh_recv, zeros_slab, (0, -1)),
            (xe_recv, zeros_edge, (1, 0)),
            (xh_recv, zeros_edge, (-1, 0)),
        ):

            @pl.when(jnp.logical_not(has[side]))
            def _():
                for k in range(2):
                    refs[s, k] = shape

        for ref, side in ((d1_recv, (1, -1)), (d2_recv, (-1, 1))):

            @pl.when(jnp.logical_not(has[side]))
            def _():
                ref[s] = zeros_edge

    def frame(ref, i, j):
        xs = {-1: (0, EDGE), 0: (EDGE, rows_x), 1: (EDGE + rows_x, EDGE)}[i]
        ys = {-1: range(WIDTH), 0: range(WIDTH, WIDTH + rows_y), 1: range(WIDTH + rows_y, 2 * WIDTH + rows_y)}[j]
        return xs, ys

    ones_slab = jnp.ones((rows_x, 128), jnp.float32)
    over_rows(lambda y: covered.__setitem__((own(y + WIDTH), slice(None)), ones_slab))
    for i, j in SIDES:
        xs, ys = frame(covered, i, j)
        inside = jnp.where(has[i, j], jnp.float32(1.0), jnp.float32(0.0))
        filler = jnp.zeros((xs[1], 128), jnp.float32) + inside
        for y in ys:
            covered[rows(y, *xs), :] = filler

    for k in range(2):
        for refs, side in ((xf_recv.at[k], (2 * k - 1, 0)), (yf_recv.at[k], (0, 2 * k - 1))):

            @pl.when(jnp.logical_not(has[side]))
            def _():
                refs[...] = jnp.zeros(refs.shape, jnp.float32)

        for j in range(2):

            @pl.when(jnp.logical_not(has[2 * k - 1, 2 * j - 1]))
            def _():
                cf_recv[k, j] = jnp.zeros((WIDTH, EDGE, 128), jnp.float32)

    loads[7].wait()
    radii = v_radius[...].astype(jnp.float32)
    for y in range(rows_y):
        weight_radius[y] = jnp.broadcast_to(radii[:, y : y + 1], (rows_x, 128))

    distances = sorted({a * a + b * b for a in range(RMAX) for b in range(RMAX) if a * a + b * b < RMAX * RMAX})

    def filtered_sum(ref, emit):
        def pair(y):
            for a in range(1, RMAX):
                sums[a - 1, y] = (
                    ref[rows(y, EDGE + a), :] + ref[rows(y, EDGE - a), :]
                )

        over_rows(pair, rows_y + 2 * WIDTH)

        def gather(y):
            def column(a, b):
                if a == 0:
                    return ref[own(y + WIDTH + b), :]
                return sums[a - 1, y + WIDTH + b]

            by_distance = {}
            for a in range(RMAX):
                for b in range(RMAX):
                    d = a * a + b * b
                    if d not in distances:
                        continue
                    term = column(a, 0) if b == 0 else column(a, b) + column(a, -b)
                    by_distance[d] = by_distance[d] + term if d in by_distance else term
            radius = weight_radius[y]
            total = radius * by_distance[0]
            for d in distances[1:]:
                total = total + jnp.maximum(radius - math.sqrt(d), 0.0) * by_distance[d]
            emit(y, total)

        over_rows(gather)

    filtered_sum(covered, lambda y, total: inv_denom.__setitem__(y, 1.0 / total))

    for load in loads[:7]:
        load.wait()

    def native(ref, y):
        return ref[pl.ds(y, rows_x, stride=rows_y), :]

    def stage(y):
        for c in range(3):
            efield[0, c, own(y), :] = native(v_electric.at[ORDER[c]], y)
        inv_eps[y] = 1.0 / (1.0 + (EPS_MATERIAL - 1.0) * native(v_density, y))

    over_rows(stage)

    def column_of(ref, x, first):
        return ref.at[pl.ds(first * slab + EDGE + x, rows_y, stride=slab), :]

    behind_mask_x = jnp.where(has[-1, 0], jnp.float32(COURANT), jnp.float32(0.0))
    behind_mask_y = jnp.where(has[0, -1], jnp.float32(COURANT), jnp.float32(0.0))

    def copies(s):
        base = 6 * s

        def copy(k, src, dst, side):
            return pltpu.make_async_remote_copy(
                src_ref=src,
                dst_ref=dst,
                send_sem=send_sems.at[base + k],
                recv_sem=recv_sems.at[base + k],
                device_id=device(*side),
                device_id_type=MESH,
            )

        return [
            ((-1, 0), copy(0, xe_send.at[s], xe_recv.at[s], (-1, 0))),
            ((1, 0), copy(1, xh_send.at[s], xh_recv.at[s], (1, 0))),
            ((0, -1), copy(2, efield.at[s, 0:2, own(0), :], ye_recv.at[s], (0, -1))),
            ((0, 1), copy(3, yh_send.at[s], yh_recv.at[s], (0, 1))),
            ((-1, 1), copy(4, xe_send.at[s, 1], d1_recv.at[s], (-1, 1))),
            (
                (1, -1),
                copy(
                    5,
                    efield.at[s, 0, edge(0, rows_x), :],
                    d2_recv.at[s],
                    (1, -1),
                ),
            ),
        ]

    def start(pairs):
        for side, copy in pairs:
            pl.when(has[side])(copy.start)

    def arrive(pairs):
        for (i, j), copy in pairs:
            pl.when(has[-i, -j])(copy.wait_recv)

    def sent(pairs):
        for side, copy in pairs:
            pl.when(has[side])(copy.wait_send)

    pending = []
    for s in range(STEPS):

        def curl_e(y, s=s):
            ex, ez, ey = (efield[s, c, own(y), :] for c in range(3))
            ex_y, ez_y = (efield[s, c, own(y + 1), :] for c in (0, 1))
            ez_x, ey_x = (efield[s, c, rows(y, EDGE + 1), :] for c in (1, 2))
            if s == 0:
                hx, hz, hy = (native(v_magnetic.at[ORDER[c]], y) for c in range(3))
            else:
                hx, hz, hy = (hfield[s - 1, c, own(y + 1), :] for c in range(3))
            hfield[s, 0, own(y + 1), :] = hx - COURANT * ((ez_y - ez) - (ahead_z(ey) - ey))
            hfield[s, 2, own(y + 1), :] = hy - COURANT * ((ahead_z(ex) - ex) - (ez_x - ez))
            hfield[s, 1, own(y + 1), :] = hz - COURANT * ((ey_x - ey) - (ex_y - ex))

        over_rows(curl_e)
        for k in range(2):
            xe_send[s, k] = column_of(efield.at[s, 1 + k], 0, 0)[...]
            xh_send[s, k] = column_of(hfield.at[s, 1 + k], rows_x - 1, 1)[...]
            yh_send[s, k] = hfield[s, k, own(rows_y), :]

        if s == 0:
            pl.semaphore_wait(barrier, greeted)
        pairs = copies(s)
        start(pairs)
        arrive(pairs)
        pending += pairs

        hfield[s, 0, own(rows_y), :] = hfield[s, 0, own(rows_y), :] - COURANT * ye_recv[s, 1]
        hfield[s, 1, own(rows_y), :] = hfield[s, 1, own(rows_y), :] + COURANT * ye_recv[s, 0]
        last_z = column_of(hfield.at[s, 1], rows_x - 1, 1)
        last_y = column_of(hfield.at[s, 2], rows_x - 1, 1)
        last_z[...] = last_z[...] - COURANT * xe_recv[s, 1]
        last_y[...] = last_y[...] + COURANT * xe_recv[s, 0]
        hfield[s, 0, own(0), :] = yh_recv[s, 0] - behind_mask_y * efield[s, 1, own(0), :]
        hfield[s, 1, own(0), :] = yh_recv[s, 1] + behind_mask_y * efield[s, 0, own(0), :]
        corner = hfield[s, 1, rows(0, EDGE + rows_x - 1, 1), :]
        hfield[s, 1, rows(0, EDGE + rows_x - 1, 1), :] = corner - COURANT * d1_recv[s, rows_y - 1 : rows_y, :]
        row = lax.broadcasted_iota(jnp.int32, (rows_y, 128), 0)
        extra = jnp.where(row == rows_y - 1, d2_recv[s, EDGE - 1 : EDGE, :], 0.0)
        column_of(hfield.at[s, 1], -1, 1)[...] = xh_recv[s, 0] - behind_mask_x * xe_send[s, 1] + COURANT * extra
        column_of(hfield.at[s, 2], -1, 1)[...] = xh_recv[s, 1] + behind_mask_x * xe_send[s, 0]

        def curl_h(y, s=s):
            hx, hz, hy = (hfield[s, c, own(y + 1), :] for c in range(3))
            hx_y, hz_y = (hfield[s, c, own(y), :] for c in (0, 1))
            hz_x, hy_x = (hfield[s, c, rows(y + 1, EDGE - 1), :] for c in (1, 2))
            curls = (
                (hz - hz_y) - (hy - behind_z(hy)),
                (hy - hy_x) - (hx - hx_y),
                (hx - behind_z(hx)) - (hz - hz_x),
            )
            material = native(v_density, y)
            scale = inv_eps[y]
            total = None
            for c in range(3):
                e = efield[s, c, own(y), :]
                if s == 0:
                    p, q = native(v_polar.at[ORDER[c]], y), native(v_rate.at[ORDER[c]], y)
                else:
                    p, q = polar[c, y], rate[c, y]
                q = DAMPING * q - OMEGA_SQUARED * p + (OMEGA_SQUARED * LORENTZ_STRENGTH) * material * e
                e = e + (COURANT * curls[c] - q) * scale
                if s + 1 < STEPS:
                    polar[c, y] = p + q
                    rate[c, y] = q
                    efield[s + 1, c, own(y), :] = e
                else:
                    o_electric[ORDER[c], pl.ds(y, rows_x, stride=rows_y), :] = e
                    o_magnetic[ORDER[c], pl.ds(y, rows_x, stride=rows_y), :] = (hx, hz, hy)[c]
                term = e * native(v_forward.at[3 * s + ORDER[c]], y)
                total = term if total is None else total + term
            if s == 0:
                gradient[y] = total
            else:
                total = gradient[y] + total
                gradient[y] = total
            if s + 1 == STEPS:
                g_send[pl.ds(y, rows_x, stride=rows_y), :] = total

        over_rows(curl_h)

    flip = pltpu.make_async_remote_copy(
        src_ref=g_send,
        dst_ref=g_recv,
        send_sem=send_sems.at[12],
        recv_sem=recv_sems.at[12],
        device_id=mirror,
        device_id_type=MESH,
    )
    flip.start()
    stores = [
        pltpu.make_async_copy(o_electric, electric_out, out_sems.at[0]),
        pltpu.make_async_copy(o_magnetic, magnetic_out, out_sems.at[1]),
        pltpu.make_async_copy(o_density, density_out, out_sems.at[2]),
    ]
    stores[0].start()
    stores[1].start()
    flip.wait_recv()

    def turn(x):
        g_flip[pl.ds(pl.multiple_of(x * rows_y, rows_y), rows_y), :] = g_recv[
            pl.ds(pl.multiple_of((rows_x - 1 - x) * rows_y, rows_y), rows_y), :
        ]

    over_rows(turn, rows_x)

    def update(y):
        mirrored = g_flip[pl.ds(partner_in[y], rows_x, stride=rows_y), :]
        symmetric = 0.5 * (gradient[y] + mirrored)
        design = native(v_mask, y).astype(jnp.float32)
        updated[own(y + WIDTH), :] = native(v_density, y) - UPDATE_STEP * design * symmetric

    over_rows(update)

    for r in range(WIDTH):
        xf_send[0, r] = column_of(updated, r, WIDTH)[...]
        xf_send[1, r] = column_of(updated, rows_x - WIDTH + r, WIDTH)[...]
        yf_send[0, r] = updated[own(WIDTH + r), :]
        yf_send[1, r] = updated[own(rows_y + r), :]

    halos = []
    for k, (i, j) in enumerate(SIDES):
        if j == 0:
            src, dst = xf_send.at[(i + 1) // 2], xf_recv.at[(1 - i) // 2]
        elif i == 0:
            src, dst = yf_send.at[(j + 1) // 2], yf_recv.at[(1 - j) // 2]
        else:
            xs = slice(0, EDGE) if i < 0 else slice(rows_x - EDGE, rows_x)
            src, dst = yf_send.at[(j + 1) // 2, :, xs, :], cf_recv.at[(1 - i) // 2, (1 - j) // 2]
        halos.append(
            (
                (i, j),
                pltpu.make_async_remote_copy(
                    src_ref=src,
                    dst_ref=dst,
                    send_sem=send_sems.at[13 + k],
                    recv_sem=recv_sems.at[13 + k],
                    device_id=device(i, j),
                    device_id_type=MESH,
                ),
            )
        )
    start(halos)
    arrive(halos)
    for r in range(WIDTH):
        column_of(updated, r - WIDTH, WIDTH)[...] = xf_recv[0, r]
        column_of(updated, rows_x + r, WIDTH)[...] = xf_recv[1, r]
        for j in range(2):
            y = r + j * (WIDTH + rows_y)
            updated[own(y), :] = yf_recv[j, r]
            updated[edge(y, 0), :] = cf_recv[0, j, r]
            updated[edge(y, EDGE + rows_x), :] = cf_recv[1, j, r]

    top = math.tanh(SHARPNESS * THRESHOLD)
    bottom = top + math.tanh(SHARPNESS * (1.0 - THRESHOLD))

    def project(y, total):
        filtered = total * inv_denom[y]
        o_density[pl.ds(y, rows_x, stride=rows_y), :] = (
            top + jnp.tanh(SHARPNESS * (filtered - THRESHOLD))
        ) / bottom

    filtered_sum(updated, project)
    stores[2].start()
    sent(pending)
    flip.wait_send()
    sent(halos)
    for store in stores:
        store.wait()


def local(nx, ny, *args):
    rows_x, rows_y, depth = args[4].shape
    cells = rows_x * rows_y
    slab = rows_x + 2 * EDGE
    f32 = jnp.float32

    def vmem(*shape, dtype=f32):
        return pltpu.VMEM(shape, dtype)

    any_spec = pl.BlockSpec(memory_space=pl.ANY)
    electric, magnetic, polar, rate, density, forward, mask, partner, radius = args
    operands = (
        electric.reshape(3, cells, depth),
        magnetic.reshape(3, cells, depth),
        polar.reshape(3, cells, depth),
        rate.reshape(3, cells, depth),
        density.reshape(cells, depth),
        forward.reshape(3 * STEPS, cells, depth),
        mask.reshape(cells, depth),
        partner,
        radius,
    )
    in_specs = [any_spec] * 7 + [pl.BlockSpec(memory_space=pltpu.SMEM), any_spec]
    outs = pl.pallas_call(
        functools.partial(kernel, nx, ny),
        out_shape=(
            jax.ShapeDtypeStruct((3, cells, depth), f32),
            jax.ShapeDtypeStruct((3, cells, depth), f32),
            jax.ShapeDtypeStruct((cells, depth), f32),
        ),
        in_specs=in_specs,
        out_specs=(any_spec, any_spec, any_spec),
        scratch_shapes=[
            vmem(3, cells, depth),
            vmem(3, cells, depth),
            vmem(3, cells, depth),
            vmem(3, cells, depth),
            vmem(cells, depth),
            vmem(3 * STEPS, cells, depth),
            vmem(cells, depth, dtype=jnp.int32),
            vmem(rows_x, rows_y, dtype=jnp.int32),
            vmem(STEPS, 3, (rows_y + 1) * slab, depth),
            vmem(STEPS, 3, (rows_y + 1) * slab, depth),
            vmem(3, rows_y, rows_x, depth),
            vmem(3, rows_y, rows_x, depth),
            vmem(rows_y, rows_x, depth),
            vmem(rows_y, rows_x, depth),
            vmem(cells, depth),
            vmem(cells, depth),
            vmem(cells, depth),
            vmem((rows_y + 2 * WIDTH) * slab, depth),
            vmem((rows_y + 2 * WIDTH) * slab, depth),
            vmem(WIDTH, rows_y + 2 * WIDTH, rows_x, depth),
            vmem(rows_y, rows_x, depth),
            vmem(rows_y, rows_x, depth),
            vmem(STEPS, 2, rows_x, depth),
            vmem(STEPS, 2, rows_x, depth),
            vmem(STEPS, 2, rows_x, depth),
            vmem(STEPS, 2, rows_y, depth),
            vmem(STEPS, 2, rows_y, depth),
            vmem(STEPS, 2, rows_y, depth),
            vmem(STEPS, 2, rows_y, depth),
            vmem(STEPS, EDGE, depth),
            vmem(STEPS, EDGE, depth),
            vmem(2, WIDTH, rows_y, depth),
            vmem(2, WIDTH, rows_y, depth),
            vmem(2, WIDTH, rows_x, depth),
            vmem(2, WIDTH, rows_x, depth),
            vmem(2, 2, WIDTH, EDGE, depth),
            vmem(3, cells, depth),
            vmem(3, cells, depth),
            vmem(cells, depth),
            pltpu.SemaphoreType.DMA((8,)),
            pltpu.SemaphoreType.DMA((3,)),
            pltpu.SemaphoreType.DMA((21,)),
            pltpu.SemaphoreType.DMA((21,)),
        ],
        compiler_params=pltpu.CompilerParams(collective_id=0, has_side_effects=True),
    )(*operands)
    return (
        outs[0].reshape(electric.shape),
        outs[1].reshape(magnetic.shape),
        outs[2].reshape(density.shape),
    )


def solution(mesh):
    in_specs = (
        P(None, "gx", "gy", None),
        P(None, "gx", "gy", None),
        P(None, "gx", "gy", None),
        P(None, "gx", "gy", None),
        P("gx", "gy", None),
        P(None, None, "gx", "gy", None),
        P("gx", "gy", None),
        P("gy"),
        P("gx", "gy"),
    )
    out_specs = (P(None, "gx", "gy", None), P(None, "gx", "gy", None), P("gx", "gy", None))
    return jax.shard_map(
        functools.partial(local, mesh.shape["gx"], mesh.shape["gy"]),
        mesh=mesh,
        in_specs=in_specs,
        out_specs=out_specs,
        check_vma=False,
    )
```

```python
import functools
import math

import jax
import jax.numpy as jnp
from jax import lax
from jax.experimental import pallas as pl
from jax.experimental.pallas import tpu as pltpu
from jax.sharding import PartitionSpec as P

STEPS = 2
RMAX = 4
COURANT = 0.5
DAMPING = 0.9
OMEGA_SQUARED = 0.3
LORENTZ_STRENGTH = 2.0
EPS_MATERIAL = 4.0
UPDATE_STEP = 0.25
SHARPNESS = 4.0
THRESHOLD = 0.5

MESH = pl.DeviceIdType.MESH
WIDTH = RMAX - 1
EDGE = 8
ORDER = (0, 2, 1)
SIDES = tuple((i, j) for i in (-1, 0, 1) for j in (-1, 0, 1) if (i, j) != (0, 0))


def kernel(
    nx,
    ny,
    electric_in,
    magnetic_in,
    polar_in,
    rate_in,
    density_in,
    forward_in,
    mask_in,
    partner_in,
    radius_in,
    o_electric,
    o_magnetic,
    o_density,
    v_electric,
    v_magnetic,
    v_polar,
    v_rate,
    v_density,
    v_forward,
    v_mask,
    v_radius,
    efield,
    hfield,
    polar,
    rate,
    driven,
    inv_eps,
    gradient,
    g_send,
    g_recv,
    g_flip,
    updated,
    covered,
    sums,
    weight_radius,
    inv_denom,
    ye_recv,
    yh_send,
    yh_recv,
    xe_send,
    xe_recv,
    xh_send,
    xh_recv,
    d1_recv,
    d2_recv,
    xf_send,
    xf_recv,
    yf_send,
    yf_recv,
    cf_recv,
    in_sems,
    send_sems,
    recv_sems,
):
    rows_y, rows_x = v_radius.shape
    slab = rows_x + 2 * EDGE

    def rows(y, first=EDGE, count=rows_x):
        return pl.ds(y * slab + first, count)

    def own(y):
        start = y * slab + EDGE
        return pl.ds(start if isinstance(start, int) else pl.multiple_of(start, EDGE), rows_x)

    def edge(y, first):
        start = y * slab + first
        return pl.ds(start if isinstance(start, int) else pl.multiple_of(start, EDGE), EDGE)

    gx, gy = lax.axis_index("gx"), lax.axis_index("gy")
    has = {}
    for i, j in SIDES:
        parts = []
        if i:
            parts.append(gx > 0 if i < 0 else gx < nx - 1)
        if j:
            parts.append(gy > 0 if j < 0 else gy < ny - 1)
        has[i, j] = functools.reduce(jnp.logical_and, parts)

    def device(i, j):
        return (lax.rem(gx + i + nx, nx), lax.rem(gy + j + ny, ny))

    mirror = (nx - 1 - gx, gy)

    loads = [
        pltpu.make_async_copy(src, dst, in_sems.at[k])
        for k, (src, dst) in enumerate(
            [
                (electric_in, v_electric),
                (magnetic_in, v_magnetic),
                (polar_in, v_polar),
                (rate_in, v_rate),
                (density_in, v_density),
                (forward_in, v_forward),
                (mask_in, v_mask),
                (radius_in, v_radius),
            ]
        )
    ]
    for load in loads:
        load.start()

    barrier = pltpu.get_barrier_semaphore()
    greeted = jnp.int32(1)
    for side in SIDES:
        greeted = greeted + has[side].astype(jnp.int32)

        @pl.when(has[side])
        def _():
            pl.semaphore_signal(barrier, inc=1, device_id=device(*side), device_id_type=MESH)

    pl.semaphore_signal(barrier, inc=1, device_id=mirror, device_id_type=MESH)

    lane = lax.broadcasted_iota(jnp.int32, (rows_x, 128), 1)

    def ahead_z(v):
        return jnp.where(lane < 127, pltpu.roll(v, 127, 1), 0.0)

    def behind_z(v):
        return jnp.where(lane > 0, pltpu.roll(v, 1, 1), 0.0)

    def over_rows(body, count=rows_y):
        def step(y, carry):
            body(y)
            return carry

        lax.fori_loop(0, count, step, 0)

    zeros_slab = jnp.zeros((rows_x, 128), jnp.float32)
    zeros_edge = jnp.zeros((EDGE, 128), jnp.float32)
    for s in range(STEPS):
        for c in range(3):
            efield[s, c, own(rows_y), :] = zeros_slab

            def clear(y, s=s, c=c):
                efield[s, c, edge(y, EDGE + rows_x), :] = zeros_edge

            over_rows(clear)

    def native(ref, y):
        return ref[pl.ds(y, rows_x, stride=rows_y), :]

    loads[0].wait()

    def stage(y):
        for c in range(3):
            efield[0, c, own(y), :] = native(v_electric.at[ORDER[c]], y)

    over_rows(stage)
    loads[1].wait()

    distances = sorted({a * a + b * b for a in range(RMAX) for b in range(RMAX) if a * a + b * b < RMAX * RMAX})

    def filtered_sum(ref, emit):
        def pair(y):
            for a in range(1, RMAX):
                sums[a - 1, y] = (
                    ref[rows(y, EDGE + a), :] + ref[rows(y, EDGE - a), :]
                )

        over_rows(pair, rows_y + 2 * WIDTH)

        def gather(y):
            def column(a, b):
                if a == 0:
                    return ref[own(y + WIDTH + b), :]
                return sums[a - 1, y + WIDTH + b]

            by_distance = {}
            for a in range(RMAX):
                for b in range(RMAX):
                    d = a * a + b * b
                    if d not in distances:
                        continue
                    term = column(a, 0) if b == 0 else column(a, b) + column(a, -b)
                    by_distance[d] = by_distance[d] + term if d in by_distance else term
            radius = weight_radius[y]
            total = radius * by_distance[0]
            for d in distances[1:]:
                total = total + jnp.maximum(radius - math.sqrt(d), 0.0) * by_distance[d]
            emit(y, total)

        over_rows(gather)

    def settle():
        for s in range(STEPS):
            for refs, shape, side in (
                (ye_recv, zeros_slab, (0, 1)),
                (yh_recv, zeros_slab, (0, -1)),
                (xe_recv, zeros_edge, (1, 0)),
                (xh_recv, zeros_edge, (-1, 0)),
            ):

                @pl.when(jnp.logical_not(has[side]))
                def _():
                    for k in range(2):
                        refs[s, k] = shape

            for ref, side in ((d1_recv, (1, -1)), (d2_recv, (-1, 1))):

                @pl.when(jnp.logical_not(has[side]))
                def _():
                    ref[s] = zeros_edge

        def frame(ref, i, j):
            xs = {-1: (0, EDGE), 0: (EDGE, rows_x), 1: (EDGE + rows_x, EDGE)}[i]
            ys = {-1: range(WIDTH), 0: range(WIDTH, WIDTH + rows_y), 1: range(WIDTH + rows_y, 2 * WIDTH + rows_y)}[j]
            return xs, ys

        ones_slab = jnp.ones((rows_x, 128), jnp.float32)
        over_rows(lambda y: covered.__setitem__((own(y + WIDTH), slice(None)), ones_slab))
        for i, j in SIDES:
            xs, ys = frame(covered, i, j)
            inside = jnp.where(has[i, j], jnp.float32(1.0), jnp.float32(0.0))
            filler = jnp.zeros((xs[1], 128), jnp.float32) + inside
            for y in ys:
                covered[rows(y, *xs), :] = filler

        for k in range(2):
            for refs, side in ((xf_recv.at[k], (2 * k - 1, 0)), (yf_recv.at[k], (0, 2 * k - 1))):

                @pl.when(jnp.logical_not(has[side]))
                def _():
                    refs[...] = jnp.zeros(refs.shape, jnp.float32)

            for j in range(2):

                @pl.when(jnp.logical_not(has[2 * k - 1, 2 * j - 1]))
                def _():
                    cf_recv[k, j] = jnp.zeros((WIDTH, EDGE, 128), jnp.float32)

        loads[7].wait()
        radii = v_radius[...].astype(jnp.float32).T
        for y in range(rows_y):
            weight_radius[y] = jnp.broadcast_to(radii[:, y : y + 1], (rows_x, 128))

        filtered_sum(covered, lambda y, total: inv_denom.__setitem__(y, 1.0 / total))
        for load in loads[2:7]:
            load.wait()

    def column_of(ref, x, first):
        return ref.at[pl.ds(first * slab + EDGE + x, rows_y, stride=slab), :]

    behind_mask_x = jnp.where(has[-1, 0], jnp.float32(COURANT), jnp.float32(0.0))
    behind_mask_y = jnp.where(has[0, -1], jnp.float32(COURANT), jnp.float32(0.0))

    def copies(s):
        base = 6 * s

        def copy(k, src, dst, side):
            return pltpu.make_async_remote_copy(
                src_ref=src,
                dst_ref=dst,
                send_sem=send_sems.at[base + k],
                recv_sem=recv_sems.at[base + k],
                device_id=device(*side),
                device_id_type=MESH,
            )

        return [
            ((-1, 0), copy(0, xe_send.at[s], xe_recv.at[s], (-1, 0))),
            ((1, 0), copy(1, xh_send.at[s], xh_recv.at[s], (1, 0))),
            ((0, -1), copy(2, efield.at[s, 0:2, own(0), :], ye_recv.at[s], (0, -1))),
            ((0, 1), copy(3, yh_send.at[s], yh_recv.at[s], (0, 1))),
            ((-1, 1), copy(4, xe_send.at[s, 1], d1_recv.at[s], (-1, 1))),
            (
                (1, -1),
                copy(
                    5,
                    efield.at[s, 0, edge(0, rows_x), :],
                    d2_recv.at[s],
                    (1, -1),
                ),
            ),
        ]

    def start(pairs):
        for side, copy in pairs:
            pl.when(has[side])(copy.start)

    def arrive(pairs):
        for (i, j), copy in pairs:
            pl.when(has[-i, -j])(copy.wait_recv)

    def sent(pairs):
        for side, copy in pairs:
            pl.when(has[side])(copy.wait_send)

    pending = []
    for s in range(STEPS):

        def curl_e(y, s=s):
            ex, ez, ey = (efield[s, c, own(y), :] for c in range(3))
            ex_y, ez_y = (efield[s, c, own(y + 1), :] for c in (0, 1))
            ez_x, ey_x = (efield[s, c, rows(y, EDGE + 1), :] for c in (1, 2))
            if s == 0:
                hx, hz, hy = (native(v_magnetic.at[ORDER[c]], y) for c in range(3))
            else:
                hx, hz, hy = (hfield[s - 1, c, own(y + 1), :] for c in range(3))
            hfield[s, 0, own(y + 1), :] = hx - COURANT * ((ez_y - ez) - (ahead_z(ey) - ey))
            hfield[s, 2, own(y + 1), :] = hy - COURANT * ((ahead_z(ex) - ex) - (ez_x - ez))
            hfield[s, 1, own(y + 1), :] = hz - COURANT * ((ey_x - ey) - (ex_y - ex))

        over_rows(curl_e)
        for k in range(2):
            xe_send[s, k] = column_of(efield.at[s, 1 + k], 0, 0)[...]
            xh_send[s, k] = column_of(hfield.at[s, 1 + k], rows_x - 1, 1)[...]
            yh_send[s, k] = hfield[s, k, own(rows_y), :]

        if s == 0:
            pl.semaphore_wait(barrier, greeted)
        pairs = copies(s)
        start(pairs)
        if s == 0:
            settle()

        def drive(y, s=s):
            if s == 0:
                inv_eps[y] = 1.0 / (1.0 + (EPS_MATERIAL - 1.0) * native(v_density, y))
            material = (OMEGA_SQUARED * LORENTZ_STRENGTH) * native(v_density, y)
            scale = inv_eps[y]
            for c in range(3):
                e = efield[s, c, own(y), :]
                if s == 0:
                    p, q = native(v_polar.at[ORDER[c]], y), native(v_rate.at[ORDER[c]], y)
                else:
                    p, q = polar[c, y], rate[c, y]
                q = DAMPING * q - OMEGA_SQUARED * p + material * e
                if s + 1 < STEPS:
                    polar[c, y] = p + q
                    rate[c, y] = q
                driven[c, y] = e - q * scale

        over_rows(drive)
        arrive(pairs)
        pending += pairs

        hfield[s, 0, own(rows_y), :] = hfield[s, 0, own(rows_y), :] - COURANT * ye_recv[s, 1]
        hfield[s, 1, own(rows_y), :] = hfield[s, 1, own(rows_y), :] + COURANT * ye_recv[s, 0]
        last_z = column_of(hfield.at[s, 1], rows_x - 1, 1)
        last_y = column_of(hfield.at[s, 2], rows_x - 1, 1)
        last_z[...] = last_z[...] - COURANT * xe_recv[s, 1]
        last_y[...] = last_y[...] + COURANT * xe_recv[s, 0]
        hfield[s, 0, own(0), :] = yh_recv[s, 0] - behind_mask_y * efield[s, 1, own(0), :]
        hfield[s, 1, own(0), :] = yh_recv[s, 1] + behind_mask_y * efield[s, 0, own(0), :]
        corner = hfield[s, 1, rows(0, EDGE + rows_x - 1, 1), :]
        hfield[s, 1, rows(0, EDGE + rows_x - 1, 1), :] = corner - COURANT * d1_recv[s, rows_y - 1 : rows_y, :]
        row = lax.broadcasted_iota(jnp.int32, (rows_y, 128), 0)
        extra = jnp.where(row == rows_y - 1, d2_recv[s, EDGE - 1 : EDGE, :], 0.0)
        column_of(hfield.at[s, 1], -1, 1)[...] = xh_recv[s, 0] - behind_mask_x * xe_send[s, 1] + COURANT * extra
        column_of(hfield.at[s, 2], -1, 1)[...] = xh_recv[s, 1] + behind_mask_x * xe_send[s, 0]

        def curl_h(y, s=s):
            hx, hz, hy = (hfield[s, c, own(y + 1), :] for c in range(3))
            hx_y, hz_y = (hfield[s, c, own(y), :] for c in (0, 1))
            hz_x, hy_x = (hfield[s, c, rows(y + 1, EDGE - 1), :] for c in (1, 2))
            curls = (
                (hz - hz_y) - (hy - behind_z(hy)),
                (hy - hy_x) - (hx - hx_y),
                (hx - behind_z(hx)) - (hz - hz_x),
            )
            scale = COURANT * inv_eps[y]
            total = None
            for c in range(3):
                e = driven[c, y] + curls[c] * scale
                if s + 1 < STEPS:
                    efield[s + 1, c, own(y), :] = e
                else:
                    o_electric[ORDER[c], pl.ds(y, rows_x, stride=rows_y), :] = e
                    o_magnetic[ORDER[c], pl.ds(y, rows_x, stride=rows_y), :] = (hx, hz, hy)[c]
                term = e * native(v_forward.at[3 * s + ORDER[c]], y)
                total = term if total is None else total + term
            if s == 0:
                gradient[y] = total
            else:
                total = gradient[y] + total
                gradient[y] = total
            if s + 1 == STEPS:
                g_send[pl.ds(y, rows_x, stride=rows_y), :] = total

        over_rows(curl_h)

    flip = pltpu.make_async_remote_copy(
        src_ref=g_send,
        dst_ref=g_recv,
        send_sem=send_sems.at[12],
        recv_sem=recv_sems.at[12],
        device_id=mirror,
        device_id_type=MESH,
    )
    flip.start()
    flip.wait_recv()

    def turn(x):
        g_flip[pl.ds(pl.multiple_of(x * rows_y, rows_y), rows_y), :] = g_recv[
            pl.ds(pl.multiple_of((rows_x - 1 - x) * rows_y, rows_y), rows_y), :
        ]

    over_rows(turn, rows_x)

    def update(y):
        mirrored = g_flip[pl.ds(partner_in[y], rows_x, stride=rows_y), :]
        symmetric = 0.5 * (gradient[y] + mirrored)
        design = native(v_mask, y).astype(jnp.float32)
        updated[own(y + WIDTH), :] = native(v_density, y) - UPDATE_STEP * design * symmetric

    over_rows(update)

    for r in range(WIDTH):
        xf_send[0, r] = column_of(updated, r, WIDTH)[...]
        xf_send[1, r] = column_of(updated, rows_x - WIDTH + r, WIDTH)[...]
        yf_send[0, r] = updated[own(WIDTH + r), :]
        yf_send[1, r] = updated[own(rows_y + r), :]

    halos = []
    for k, (i, j) in enumerate(SIDES):
        if j == 0:
            src, dst = xf_send.at[(i + 1) // 2], xf_recv.at[(1 - i) // 2]
        elif i == 0:
            src, dst = yf_send.at[(j + 1) // 2], yf_recv.at[(1 - j) // 2]
        else:
            xs = slice(0, EDGE) if i < 0 else slice(rows_x - EDGE, rows_x)
            src, dst = yf_send.at[(j + 1) // 2, :, xs, :], cf_recv.at[(1 - i) // 2, (1 - j) // 2]
        halos.append(
            (
                (i, j),
                pltpu.make_async_remote_copy(
                    src_ref=src,
                    dst_ref=dst,
                    send_sem=send_sems.at[13 + k],
                    recv_sem=recv_sems.at[13 + k],
                    device_id=device(i, j),
                    device_id_type=MESH,
                ),
            )
        )
    start(halos)
    arrive(halos)
    for r in range(WIDTH):
        column_of(updated, r - WIDTH, WIDTH)[...] = xf_recv[0, r]
        column_of(updated, rows_x + r, WIDTH)[...] = xf_recv[1, r]
        for j in range(2):
            y = r + j * (WIDTH + rows_y)
            updated[own(y), :] = yf_recv[j, r]
            updated[edge(y, 0), :] = cf_recv[0, j, r]
            updated[edge(y, EDGE + rows_x), :] = cf_recv[1, j, r]

    top = math.tanh(SHARPNESS * THRESHOLD)
    bottom = top + math.tanh(SHARPNESS * (1.0 - THRESHOLD))

    def project(y, total):
        filtered = total * inv_denom[y]
        o_density[pl.ds(y, rows_x, stride=rows_y), :] = (
            top + jnp.tanh(SHARPNESS * (filtered - THRESHOLD))
        ) / bottom

    filtered_sum(updated, project)
    sent(pending)
    flip.wait_send()
    sent(halos)


def write_out(electric, magnetic, density, electric_out, magnetic_out, density_out, sems):
    pairs = ((electric, electric_out), (magnetic, magnetic_out), (density, density_out))
    stores = [pltpu.make_async_copy(src, dst, sems.at[k]) for k, (src, dst) in enumerate(pairs)]
    for store in stores:
        store.start()
    for store in stores:
        store.wait()


def local(nx, ny, *args):
    rows_x, rows_y, depth = args[4].shape
    cells = rows_x * rows_y
    slab = rows_x + 2 * EDGE
    f32 = jnp.float32

    def vmem(*shape, dtype=f32):
        return pltpu.VMEM(shape, dtype)

    any_spec = pl.BlockSpec(memory_space=pl.ANY)
    electric, magnetic, polar, rate, density, forward, mask, partner, radius = args
    operands = (
        electric.reshape(3, cells, depth),
        magnetic.reshape(3, cells, depth),
        polar.reshape(3, cells, depth),
        rate.reshape(3, cells, depth),
        density.reshape(cells, depth),
        forward.reshape(3 * STEPS, cells, depth),
        mask.reshape(cells, depth),
        partner,
        radius.T,
    )
    in_specs = [any_spec] * 7 + [pl.BlockSpec(memory_space=pltpu.SMEM), any_spec]
    shapes = ((3, cells, depth), (3, cells, depth), (cells, depth))
    vmem_spec = pl.BlockSpec(memory_space=pltpu.VMEM)
    held = pl.pallas_call(
        functools.partial(kernel, nx, ny),
        out_shape=tuple(pltpu.VMEM(shape, f32) for shape in shapes),
        in_specs=in_specs,
        out_specs=(vmem_spec,) * 3,
        scratch_shapes=[
            vmem(3, cells, depth),
            vmem(3, cells, depth),
            vmem(3, cells, depth),
            vmem(3, cells, depth),
            vmem(cells, depth),
            vmem(3 * STEPS, cells, depth),
            vmem(cells, depth, dtype=jnp.int32),
            vmem(rows_y, rows_x, dtype=jnp.int32),
            vmem(STEPS, 3, (rows_y + 1) * slab, depth),
            vmem(STEPS, 3, (rows_y + 1) * slab, depth),
            vmem(3, rows_y, rows_x, depth),
            vmem(3, rows_y, rows_x, depth),
            vmem(3, rows_y, rows_x, depth),
            vmem(rows_y, rows_x, depth),
            vmem(rows_y, rows_x, depth),
            vmem(cells, depth),
            vmem(cells, depth),
            vmem(cells, depth),
            vmem((rows_y + 2 * WIDTH) * slab, depth),
            vmem((rows_y + 2 * WIDTH) * slab, depth),
            vmem(WIDTH, rows_y + 2 * WIDTH, rows_x, depth),
            vmem(rows_y, rows_x, depth),
            vmem(rows_y, rows_x, depth),
            vmem(STEPS, 2, rows_x, depth),
            vmem(STEPS, 2, rows_x, depth),
            vmem(STEPS, 2, rows_x, depth),
            vmem(STEPS, 2, rows_y, depth),
            vmem(STEPS, 2, rows_y, depth),
            vmem(STEPS, 2, rows_y, depth),
            vmem(STEPS, 2, rows_y, depth),
            vmem(STEPS, EDGE, depth),
            vmem(STEPS, EDGE, depth),
            vmem(2, WIDTH, rows_y, depth),
            vmem(2, WIDTH, rows_y, depth),
            vmem(2, WIDTH, rows_x, depth),
            vmem(2, WIDTH, rows_x, depth),
            vmem(2, 2, WIDTH, EDGE, depth),
            pltpu.SemaphoreType.DMA((8,)),
            pltpu.SemaphoreType.DMA((21,)),
            pltpu.SemaphoreType.DMA((21,)),
        ],
        compiler_params=pltpu.CompilerParams(collective_id=0, has_side_effects=True),
    )(*operands)
    outs = pl.pallas_call(
        write_out,
        out_shape=tuple(jax.ShapeDtypeStruct(shape, f32) for shape in shapes),
        in_specs=[vmem_spec] * 3,
        out_specs=(any_spec,) * 3,
        scratch_shapes=[pltpu.SemaphoreType.DMA((3,))],
    )(*[pltpu.with_memory_space_constraint(a, pltpu.VMEM) for a in held])
    return (
        outs[0].reshape(electric.shape),
        outs[1].reshape(magnetic.shape),
        outs[2].reshape(density.shape),
    )


def solution(mesh):
    in_specs = (
        P(None, "gx", "gy", None),
        P(None, "gx", "gy", None),
        P(None, "gx", "gy", None),
        P(None, "gx", "gy", None),
        P("gx", "gy", None),
        P(None, None, "gx", "gy", None),
        P("gx", "gy", None),
        P("gy"),
        P("gx", "gy"),
    )
    out_specs = (P(None, "gx", "gy", None), P(None, "gx", "gy", None), P("gx", "gy", None))
    return jax.shard_map(
        functools.partial(local, mesh.shape["gx"], mesh.shape["gy"]),
        mesh=mesh,
        in_specs=in_specs,
        out_specs=out_specs,
        check_vma=False,
    )
```

```python
import functools
import math

import jax
import jax.numpy as jnp
from jax import lax
from jax.experimental import pallas as pl
from jax.experimental.pallas import tpu as pltpu
from jax.sharding import PartitionSpec as P

STEPS = 2
RMAX = 4
COURANT = 0.5
DAMPING = 0.9
OMEGA_SQUARED = 0.3
LORENTZ_STRENGTH = 2.0
EPS_MATERIAL = 4.0
UPDATE_STEP = 0.25
SHARPNESS = 4.0
THRESHOLD = 0.5

MESH = pl.DeviceIdType.MESH
WIDTH = RMAX - 1
EDGE = 8
ORDER = (0, 2, 1)
SIDES = tuple((i, j) for i in (-1, 0, 1) for j in (-1, 0, 1) if (i, j) != (0, 0))


def kernel(
    nx,
    ny,
    electric_in,
    magnetic_in,
    polar_in,
    rate_in,
    density_in,
    forward_in,
    mask_in,
    partner_in,
    radius_in,
    o_electric,
    o_magnetic,
    o_density,
    v_electric,
    v_magnetic,
    v_polar,
    v_rate,
    v_density,
    v_forward,
    v_mask,
    v_radius,
    efield,
    hfield,
    polar,
    rate,
    driven,
    kept,
    inv_eps,
    gradient,
    g_send,
    g_recv,
    g_turn,
    g_flip,
    ends_send,
    ends_recv,
    updated,
    covered,
    sums,
    weight_radius,
    inv_denom,
    ye_recv,
    yh_send,
    yh_recv,
    xe_send,
    xe_recv,
    xh_send,
    xh_recv,
    d1_recv,
    d2_recv,
    xf_send,
    xf_recv,
    yf_send,
    yf_recv,
    cf_recv,
    in_sems,
    send_sems,
    recv_sems,
):
    rows_y, rows_x = v_radius.shape
    slab = rows_x + 2 * EDGE

    def rows(y, first=EDGE, count=rows_x):
        return pl.ds(y * slab + first, count)

    def own(y):
        start = y * slab + EDGE
        return pl.ds(start if isinstance(start, int) else pl.multiple_of(start, EDGE), rows_x)

    def edge(y, first):
        start = y * slab + first
        return pl.ds(start if isinstance(start, int) else pl.multiple_of(start, EDGE), EDGE)

    gx, gy = lax.axis_index("gx"), lax.axis_index("gy")
    has = {}
    for i, j in SIDES:
        parts = []
        if i:
            parts.append(gx > 0 if i < 0 else gx < nx - 1)
        if j:
            parts.append(gy > 0 if j < 0 else gy < ny - 1)
        has[i, j] = functools.reduce(jnp.logical_and, parts)

    def device(i, j):
        return (lax.rem(gx + i + nx, nx), lax.rem(gy + j + ny, ny))

    mirror = (nx - 1 - gx, gy)

    loads = [
        pltpu.make_async_copy(src, dst, in_sems.at[k])
        for k, (src, dst) in enumerate(
            [
                (electric_in, v_electric),
                (magnetic_in, v_magnetic),
                (polar_in, v_polar),
                (rate_in, v_rate),
                (density_in, v_density),
                (forward_in, v_forward),
                (mask_in, v_mask),
                (radius_in, v_radius),
            ]
        )
    ]
    for load in loads:
        load.start()

    barrier = pltpu.get_barrier_semaphore()
    greeted = jnp.int32(1)
    for side in SIDES:
        greeted = greeted + has[side].astype(jnp.int32)

        @pl.when(has[side])
        def _():
            pl.semaphore_signal(barrier, inc=1, device_id=device(*side), device_id_type=MESH)

    pl.semaphore_signal(barrier, inc=1, device_id=mirror, device_id_type=MESH)

    lane = lax.broadcasted_iota(jnp.int32, (rows_x, 128), 1)

    def ahead_z(v):
        return jnp.where(lane < 127, pltpu.roll(v, 127, 1), 0.0)

    def behind_z(v):
        return jnp.where(lane > 0, pltpu.roll(v, 1, 1), 0.0)

    def over_rows(body, stop=rows_y, start=0):
        def step(y, carry):
            body(y)
            return carry

        lax.fori_loop(start, stop, step, 0)

    zeros_slab = jnp.zeros((rows_x, 128), jnp.float32)
    zeros_edge = jnp.zeros((EDGE, 128), jnp.float32)
    for s in range(STEPS):
        for c in range(3):
            efield[s, c, own(rows_y), :] = zeros_slab

            def clear(y, s=s, c=c):
                efield[s, c, edge(y, EDGE + rows_x), :] = zeros_edge

            over_rows(clear)

    def native(ref, y):
        return ref[pl.ds(y, rows_x, stride=rows_y), :]

    loads[0].wait()

    def stage(y):
        for c in range(3):
            efield[0, c, own(y), :] = native(v_electric.at[ORDER[c]], y)

    over_rows(stage)
    loads[1].wait()

    distances = sorted({a * a + b * b for a in range(RMAX) for b in range(RMAX) if a * a + b * b < RMAX * RMAX})

    def filtered_sum(ref, emit):
        def pair(y):
            for a in range(1, RMAX):
                sums[a - 1, y] = (
                    ref[rows(y, EDGE + a), :] + ref[rows(y, EDGE - a), :]
                )

        over_rows(pair, rows_y + 2 * WIDTH)

        def gather(y):
            def column(a, b):
                if a == 0:
                    return ref[own(y + WIDTH + b), :]
                return sums[a - 1, y + WIDTH + b]

            by_distance = {}
            for a in range(RMAX):
                for b in range(RMAX):
                    d = a * a + b * b
                    if d not in distances:
                        continue
                    term = column(a, 0) if b == 0 else column(a, b) + column(a, -b)
                    by_distance[d] = by_distance[d] + term if d in by_distance else term
            radius = weight_radius[y]
            total = radius * by_distance[0]
            for d in distances[1:]:
                total = total + jnp.maximum(radius - math.sqrt(d), 0.0) * by_distance[d]
            emit(y, total)

        over_rows(gather)

    def settle():
        for s in range(STEPS):
            for refs, shape, side in (
                (ye_recv, zeros_slab, (0, 1)),
                (yh_recv, zeros_slab, (0, -1)),
                (xe_recv, zeros_edge, (1, 0)),
                (xh_recv, zeros_edge, (-1, 0)),
            ):

                @pl.when(jnp.logical_not(has[side]))
                def _():
                    for k in range(2):
                        refs[s, k] = shape

            for ref, side in ((d1_recv, (1, -1)), (d2_recv, (-1, 1))):

                @pl.when(jnp.logical_not(has[side]))
                def _():
                    ref[s] = zeros_edge

        def frame(ref, i, j):
            xs = {-1: (0, EDGE), 0: (EDGE, rows_x), 1: (EDGE + rows_x, EDGE)}[i]
            ys = {-1: range(WIDTH), 0: range(WIDTH, WIDTH + rows_y), 1: range(WIDTH + rows_y, 2 * WIDTH + rows_y)}[j]
            return xs, ys

        ones_slab = jnp.ones((rows_x, 128), jnp.float32)
        over_rows(lambda y: covered.__setitem__((own(y + WIDTH), slice(None)), ones_slab))
        for i, j in SIDES:
            xs, ys = frame(covered, i, j)
            inside = jnp.where(has[i, j], jnp.float32(1.0), jnp.float32(0.0))
            filler = jnp.zeros((xs[1], 128), jnp.float32) + inside
            for y in ys:
                covered[rows(y, *xs), :] = filler

        for k in range(2):
            for refs, side in ((xf_recv.at[k], (2 * k - 1, 0)), (yf_recv.at[k], (0, 2 * k - 1))):

                @pl.when(jnp.logical_not(has[side]))
                def _():
                    refs[...] = jnp.zeros(refs.shape, jnp.float32)

            for j in range(2):

                @pl.when(jnp.logical_not(has[2 * k - 1, 2 * j - 1]))
                def _():
                    cf_recv[k, j] = jnp.zeros((WIDTH, EDGE, 128), jnp.float32)

        loads[7].wait()
        radii = v_radius[...].astype(jnp.float32).T
        for y in range(rows_y):
            weight_radius[y] = jnp.broadcast_to(radii[:, y : y + 1], (rows_x, 128))

        filtered_sum(covered, lambda y, total: inv_denom.__setitem__(y, 1.0 / total))
        for load in loads[2:7]:
            load.wait()

    def column_of(ref, x, first):
        return ref.at[pl.ds(first * slab + EDGE + x, rows_y, stride=slab), :]

    behind_mask_x = jnp.where(has[-1, 0], jnp.float32(COURANT), jnp.float32(0.0))
    behind_mask_y = jnp.where(has[0, -1], jnp.float32(COURANT), jnp.float32(0.0))

    def copies(s):
        base = 6 * s

        def copy(k, src, dst, side):
            return pltpu.make_async_remote_copy(
                src_ref=src,
                dst_ref=dst,
                send_sem=send_sems.at[base + k],
                recv_sem=recv_sems.at[base + k],
                device_id=device(*side),
                device_id_type=MESH,
            )

        return [
            ((-1, 0), copy(0, xe_send.at[s], xe_recv.at[s], (-1, 0))),
            ((1, 0), copy(1, xh_send.at[s], xh_recv.at[s], (1, 0))),
            ((0, -1), copy(2, efield.at[s, 0:2, own(0), :], ye_recv.at[s], (0, -1))),
            ((0, 1), copy(3, yh_send.at[s], yh_recv.at[s], (0, 1))),
            ((-1, 1), copy(4, xe_send.at[s, 1], d1_recv.at[s], (-1, 1))),
            (
                (1, -1),
                copy(
                    5,
                    efield.at[s, 0, edge(0, rows_x), :],
                    d2_recv.at[s],
                    (1, -1),
                ),
            ),
        ]

    def start(pairs):
        for side, copy in pairs:
            pl.when(has[side])(copy.start)

    def arrive(pairs):
        for (i, j), copy in pairs:
            pl.when(has[-i, -j])(copy.wait_recv)

    def sent(pairs):
        for side, copy in pairs:
            pl.when(has[side])(copy.wait_send)

    def column(y):
        return pl.ds(y * rows_x if isinstance(y, int) else pl.multiple_of(y * rows_x, rows_x), rows_x)

    def curled(s, y):
        ex, ez, ey = (efield[s, c, own(y), :] for c in range(3))
        ex_y, ez_y = (efield[s, c, own(y + 1), :] for c in (0, 1))
        ez_x, ey_x = (efield[s, c, rows(y, EDGE + 1), :] for c in (1, 2))
        if s == 0:
            hx, hz, hy = (native(v_magnetic.at[ORDER[c]], y) for c in range(3))
        else:
            hx, hz, hy = (hfield[s - 1, c, own(y + 1), :] for c in range(3))
        hfield[s, 0, own(y + 1), :] = hx - COURANT * ((ez_y - ez) - (ahead_z(ey) - ey))
        hfield[s, 2, own(y + 1), :] = hy - COURANT * ((ahead_z(ex) - ex) - (ez_x - ez))
        hfield[s, 1, own(y + 1), :] = hz - COURANT * ((ey_x - ey) - (ex_y - ex))

    def driven_by(s, y, fields):
        material = (OMEGA_SQUARED * LORENTZ_STRENGTH) * native(v_density, y)
        scale = inv_eps[y]
        for c in range(3):
            if s == 0:
                p, q = native(v_polar.at[ORDER[c]], y), native(v_rate.at[ORDER[c]], y)
            else:
                p, q = polar[c, y], rate[c, y]
            q = DAMPING * q - OMEGA_SQUARED * p + material * fields[c]
            if s + 1 < STEPS:
                polar[c, y] = p + q
                rate[c, y] = q
            driven[c, y] = fields[c] - q * scale

    def advanced(s, y):
        hx, hz, hy = (hfield[s, c, own(y + 1), :] for c in range(3))
        hx_y, hz_y = (hfield[s, c, own(y), :] for c in (0, 1))
        hz_x, hy_x = (hfield[s, c, rows(y + 1, EDGE - 1), :] for c in (1, 2))
        curls = (
            (hz - hz_y) - (hy - behind_z(hy)),
            (hy - hy_x) - (hx - hx_y),
            (hx - behind_z(hx)) - (hz - hz_x),
        )
        scale = COURANT * inv_eps[y]
        news = [driven[c, y] + curls[c] * scale for c in range(3)]
        total = None
        for c in range(3):
            term = news[c] * native(v_forward.at[3 * s + ORDER[c]], y)
            total = term if total is None else total + term
        return (hx, hz, hy), news, total

    def flip(k, src, dst):
        return pltpu.make_async_remote_copy(
            src_ref=src,
            dst_ref=dst,
            send_sem=send_sems.at[k],
            recv_sem=recv_sems.at[k],
            device_id=mirror,
            device_id_type=MESH,
        )

    def inner_rows():
        def first(y):
            _, news, total = advanced(0, y)
            for c in range(3):
                efield[1, c, own(y), :] = news[c]
            gradient[column(y), :] = total

        over_rows(first, rows_y - 1, 1)
        over_rows(lambda y: curled(1, y), rows_y - 2, 1)

        def second(y):
            material = (OMEGA_SQUARED * LORENTZ_STRENGTH) * native(v_density, y)
            for c in range(3):
                kept[c, y] = driven[c, y]
                e = efield[1, c, own(y), :]
                q = DAMPING * rate[c, y] - OMEGA_SQUARED * polar[c, y] + material * e
                driven[c, y] = e - q * inv_eps[y]
            _, _, total = advanced(1, y)
            g_send[column(y), :] = gradient[column(y), :] + total
            for c in range(3):
                driven[c, y] = kept[c, y]

        over_rows(second, rows_y - 2, 2)

    inner = pl.ds(2 * rows_x, (rows_y - 4) * rows_x)
    flips = [flip(12, g_send.at[inner, :], g_recv.at[inner, :])]
    flips += [flip(13 + k, g_send.at[column(y), :], g_recv.at[column(y), :]) for k, y in enumerate((1, rows_y - 2))]
    flips += [flip(15 + k, gradient.at[column(y), :], g_recv.at[column(y), :]) for k, y in enumerate((0, rows_y - 1))]
    flips += [flip(17, ends_send, ends_recv)]
    ends = (0, 1, rows_x - 2, rows_x - 1)

    pending = []
    for s in range(STEPS):

        def curl_e(y, s=s):
            curled(s, y)

        over_rows(curl_e)
        for k in range(2):
            xe_send[s, k] = column_of(efield.at[s, 1 + k], 0, 0)[...]
            xh_send[s, k] = column_of(hfield.at[s, 1 + k], rows_x - 1, 1)[...]
            yh_send[s, k] = hfield[s, k, own(rows_y), :]

        if s == 0:
            pl.semaphore_wait(barrier, greeted)
        pairs = copies(s)
        start(pairs)
        if s == 0:
            settle()
            over_rows(
                lambda y: inv_eps.__setitem__(
                    y, 1.0 / (1.0 + (EPS_MATERIAL - 1.0) * native(v_density, y))
                )
            )

        def drive(y, s=s):
            driven_by(s, y, [efield[s, c, own(y), :] for c in range(3)])

        over_rows(drive)
        if s == 0:
            inner_rows()
            flips[0].start()
        else:
            for y in (1, rows_y - 2):
                g_send[column(y), :] = gradient[column(y), :] + advanced(s, y)[2]
            flips[1].start()
            flips[2].start()
        arrive(pairs)
        pending += pairs

        hfield[s, 0, own(rows_y), :] = hfield[s, 0, own(rows_y), :] - COURANT * ye_recv[s, 1]
        hfield[s, 1, own(rows_y), :] = hfield[s, 1, own(rows_y), :] + COURANT * ye_recv[s, 0]
        last_z = column_of(hfield.at[s, 1], rows_x - 1, 1)
        last_y = column_of(hfield.at[s, 2], rows_x - 1, 1)
        last_z[...] = last_z[...] - COURANT * xe_recv[s, 1]
        last_y[...] = last_y[...] + COURANT * xe_recv[s, 0]
        hfield[s, 0, own(0), :] = yh_recv[s, 0] - behind_mask_y * efield[s, 1, own(0), :]
        hfield[s, 1, own(0), :] = yh_recv[s, 1] + behind_mask_y * efield[s, 0, own(0), :]
        corner = hfield[s, 1, rows(0, EDGE + rows_x - 1, 1), :]
        hfield[s, 1, rows(0, EDGE + rows_x - 1, 1), :] = corner - COURANT * d1_recv[s, rows_y - 1 : rows_y, :]
        row = lax.broadcasted_iota(jnp.int32, (rows_y, 128), 0)
        extra = jnp.where(row == rows_y - 1, d2_recv[s, EDGE - 1 : EDGE, :], 0.0)
        column_of(hfield.at[s, 1], -1, 1)[...] = xh_recv[s, 0] - behind_mask_x * xe_send[s, 1] + COURANT * extra
        column_of(hfield.at[s, 2], -1, 1)[...] = xh_recv[s, 1] + behind_mask_x * xe_send[s, 0]

        def curl_h(y, s=s):
            hs, news, total = advanced(s, y)
            for c in range(3):
                if s + 1 < STEPS:
                    efield[s + 1, c, own(y), :] = news[c]
                else:
                    o_electric[ORDER[c], pl.ds(y, rows_x, stride=rows_y), :] = news[c]
                    o_magnetic[ORDER[c], pl.ds(y, rows_x, stride=rows_y), :] = hs[c]
            if s > 0:
                total = gradient[column(y), :] + total
            gradient[column(y), :] = total

        over_rows(curl_h)

    for k, x in enumerate(ends):
        ends_send[k] = gradient[pl.ds(x, rows_y, stride=rows_x), :]
    for copy in flips[3:]:
        copy.start()
    for copy in flips:
        copy.wait_recv()

    def spread(y):
        g_turn[pl.ds(y, rows_x, stride=rows_y), :] = g_recv[column(y), :]

    over_rows(spread)
    for k, x in enumerate(ends):
        g_turn[pl.ds(x * rows_y, rows_y), :] = ends_recv[k]

    def turn(x):
        g_flip[pl.ds(pl.multiple_of(x * rows_y, rows_y), rows_y), :] = g_turn[
            pl.ds(pl.multiple_of((rows_x - 1 - x) * rows_y, rows_y), rows_y), :
        ]

    over_rows(turn, rows_x)

    def update(y):
        mirrored = g_flip[pl.ds(partner_in[y], rows_x, stride=rows_y), :]
        symmetric = 0.5 * (gradient[column(y), :] + mirrored)
        design = native(v_mask, y).astype(jnp.float32)
        updated[own(y + WIDTH), :] = native(v_density, y) - UPDATE_STEP * design * symmetric

    over_rows(update)

    for r in range(WIDTH):
        xf_send[0, r] = column_of(updated, r, WIDTH)[...]
        xf_send[1, r] = column_of(updated, rows_x - WIDTH + r, WIDTH)[...]
        yf_send[0, r] = updated[own(WIDTH + r), :]
        yf_send[1, r] = updated[own(rows_y + r), :]

    halos = []
    for k, (i, j) in enumerate(SIDES):
        if j == 0:
            src, dst = xf_send.at[(i + 1) // 2], xf_recv.at[(1 - i) // 2]
        elif i == 0:
            src, dst = yf_send.at[(j + 1) // 2], yf_recv.at[(1 - j) // 2]
        else:
            xs = slice(0, EDGE) if i < 0 else slice(rows_x - EDGE, rows_x)
            src, dst = yf_send.at[(j + 1) // 2, :, xs, :], cf_recv.at[(1 - i) // 2, (1 - j) // 2]
        halos.append(
            (
                (i, j),
                pltpu.make_async_remote_copy(
                    src_ref=src,
                    dst_ref=dst,
                    send_sem=send_sems.at[18 + k],
                    recv_sem=recv_sems.at[18 + k],
                    device_id=device(i, j),
                    device_id_type=MESH,
                ),
            )
        )
    start(halos)
    arrive(halos)
    for r in range(WIDTH):
        column_of(updated, r - WIDTH, WIDTH)[...] = xf_recv[0, r]
        column_of(updated, rows_x + r, WIDTH)[...] = xf_recv[1, r]
        for j in range(2):
            y = r + j * (WIDTH + rows_y)
            updated[own(y), :] = yf_recv[j, r]
            updated[edge(y, 0), :] = cf_recv[0, j, r]
            updated[edge(y, EDGE + rows_x), :] = cf_recv[1, j, r]

    top = math.tanh(SHARPNESS * THRESHOLD)
    bottom = top + math.tanh(SHARPNESS * (1.0 - THRESHOLD))

    def project(y, total):
        filtered = total * inv_denom[y]
        o_density[pl.ds(y, rows_x, stride=rows_y), :] = (
            top + jnp.tanh(SHARPNESS * (filtered - THRESHOLD))
        ) / bottom

    filtered_sum(updated, project)
    sent(pending)
    for copy in flips:
        copy.wait_send()
    sent(halos)


def write_out(electric, magnetic, density, electric_out, magnetic_out, density_out, sems):
    pairs = ((electric, electric_out), (magnetic, magnetic_out), (density, density_out))
    stores = [pltpu.make_async_copy(src, dst, sems.at[k]) for k, (src, dst) in enumerate(pairs)]
    for store in stores:
        store.start()
    for store in stores:
        store.wait()


def local(nx, ny, *args):
    rows_x, rows_y, depth = args[4].shape
    cells = rows_x * rows_y
    slab = rows_x + 2 * EDGE
    f32 = jnp.float32

    def vmem(*shape, dtype=f32):
        return pltpu.VMEM(shape, dtype)

    any_spec = pl.BlockSpec(memory_space=pl.ANY)
    electric, magnetic, polar, rate, density, forward, mask, partner, radius = args
    operands = (
        electric.reshape(3, cells, depth),
        magnetic.reshape(3, cells, depth),
        polar.reshape(3, cells, depth),
        rate.reshape(3, cells, depth),
        density.reshape(cells, depth),
        forward.reshape(3 * STEPS, cells, depth),
        mask.reshape(cells, depth),
        partner,
        radius.T,
    )
    in_specs = [any_spec] * 7 + [pl.BlockSpec(memory_space=pltpu.SMEM), any_spec]
    shapes = ((3, cells, depth), (3, cells, depth), (cells, depth))
    vmem_spec = pl.BlockSpec(memory_space=pltpu.VMEM)
    held = pl.pallas_call(
        functools.partial(kernel, nx, ny),
        out_shape=tuple(pltpu.VMEM(shape, f32) for shape in shapes),
        in_specs=in_specs,
        out_specs=(vmem_spec,) * 3,
        scratch_shapes=[
            vmem(3, cells, depth),
            vmem(3, cells, depth),
            vmem(3, cells, depth),
            vmem(3, cells, depth),
            vmem(cells, depth),
            vmem(3 * STEPS, cells, depth),
            vmem(cells, depth, dtype=jnp.int32),
            vmem(rows_y, rows_x, dtype=jnp.int32),
            vmem(STEPS, 3, (rows_y + 1) * slab, depth),
            vmem(STEPS, 3, (rows_y + 1) * slab, depth),
            vmem(3, rows_y, rows_x, depth),
            vmem(3, rows_y, rows_x, depth),
            vmem(3, rows_y, rows_x, depth),
            vmem(3, rows_y, rows_x, depth),
            vmem(rows_y, rows_x, depth),
            vmem(cells, depth),
            vmem(cells, depth),
            vmem(cells, depth),
            vmem(cells, depth),
            vmem(cells, depth),
            vmem(4, rows_y, depth),
            vmem(4, rows_y, depth),
            vmem((rows_y + 2 * WIDTH) * slab, depth),
            vmem((rows_y + 2 * WIDTH) * slab, depth),
            vmem(WIDTH, rows_y + 2 * WIDTH, rows_x, depth),
            vmem(rows_y, rows_x, depth),
            vmem(rows_y, rows_x, depth),
            vmem(STEPS, 2, rows_x, depth),
            vmem(STEPS, 2, rows_x, depth),
            vmem(STEPS, 2, rows_x, depth),
            vmem(STEPS, 2, rows_y, depth),
            vmem(STEPS, 2, rows_y, depth),
            vmem(STEPS, 2, rows_y, depth),
            vmem(STEPS, 2, rows_y, depth),
            vmem(STEPS, EDGE, depth),
            vmem(STEPS, EDGE, depth),
            vmem(2, WIDTH, rows_y, depth),
            vmem(2, WIDTH, rows_y, depth),
            vmem(2, WIDTH, rows_x, depth),
            vmem(2, WIDTH, rows_x, depth),
            vmem(2, 2, WIDTH, EDGE, depth),
            pltpu.SemaphoreType.DMA((8,)),
            pltpu.SemaphoreType.DMA((26,)),
            pltpu.SemaphoreType.DMA((26,)),
        ],
        compiler_params=pltpu.CompilerParams(collective_id=0, has_side_effects=True),
    )(*operands)
    outs = pl.pallas_call(
        write_out,
        out_shape=tuple(jax.ShapeDtypeStruct(shape, f32) for shape in shapes),
        in_specs=[vmem_spec] * 3,
        out_specs=(any_spec,) * 3,
        scratch_shapes=[pltpu.SemaphoreType.DMA((3,))],
    )(*[pltpu.with_memory_space_constraint(a, pltpu.VMEM) for a in held])
    return (
        outs[0].reshape(electric.shape),
        outs[1].reshape(magnetic.shape),
        outs[2].reshape(density.shape),
    )


def solution(mesh):
    in_specs = (
        P(None, "gx", "gy", None),
        P(None, "gx", "gy", None),
        P(None, "gx", "gy", None),
        P(None, "gx", "gy", None),
        P("gx", "gy", None),
        P(None, None, "gx", "gy", None),
        P("gx", "gy", None),
        P("gy"),
        P("gx", "gy"),
    )
    out_specs = (P(None, "gx", "gy", None), P(None, "gx", "gy", None), P("gx", "gy", None))
    return jax.shard_map(
        functools.partial(local, mesh.shape["gx"], mesh.shape["gy"]),
        mesh=mesh,
        in_specs=in_specs,
        out_specs=out_specs,
        check_vma=False,
    )
```

```python
import functools
import math

import jax
import jax.numpy as jnp
from jax import lax
from jax.experimental import pallas as pl
from jax.experimental.pallas import tpu as pltpu
from jax.sharding import PartitionSpec as P

STEPS = 2
RMAX = 4
COURANT = 0.5
DAMPING = 0.9
OMEGA_SQUARED = 0.3
LORENTZ_STRENGTH = 2.0
EPS_MATERIAL = 4.0
UPDATE_STEP = 0.25
SHARPNESS = 4.0
THRESHOLD = 0.5

MESH = pl.DeviceIdType.MESH
WIDTH = RMAX - 1
EDGE = 8
ORDER = (0, 2, 1)
SIDES = tuple((i, j) for i in (-1, 0, 1) for j in (-1, 0, 1) if (i, j) != (0, 0))


def kernel(
    nx,
    ny,
    electric_in,
    magnetic_in,
    polar_in,
    rate_in,
    density_in,
    forward_in,
    mask_in,
    partner_in,
    radius_in,
    o_electric,
    o_magnetic,
    o_density,
    v_electric,
    v_magnetic,
    v_polar,
    v_rate,
    v_density,
    v_forward,
    v_mask,
    v_radius,
    partner,
    efield,
    hfield,
    polar,
    rate,
    driven,
    kept,
    inv_eps,
    gradient,
    g_send,
    g_recv,
    g_turn,
    g_flip,
    ends_send,
    ends_recv,
    updated,
    covered,
    sums,
    weight_radius,
    inv_denom,
    ye_recv,
    yh_send,
    yh_recv,
    xe_send,
    xe_recv,
    xh_send,
    xh_recv,
    d1_recv,
    d2_recv,
    xf_send,
    xf_recv,
    yf_send,
    yf_recv,
    cf_recv,
    in_sems,
    send_sems,
    recv_sems,
):
    rows_y, rows_x = v_radius.shape
    slab = rows_x + 2 * EDGE

    def rows(y, first=EDGE, count=rows_x):
        return pl.ds(y * slab + first, count)

    def own(y):
        start = y * slab + EDGE
        return pl.ds(start if isinstance(start, int) else pl.multiple_of(start, EDGE), rows_x)

    def edge(y, first):
        start = y * slab + first
        return pl.ds(start if isinstance(start, int) else pl.multiple_of(start, EDGE), EDGE)

    gx, gy = lax.axis_index("gx"), lax.axis_index("gy")
    has = {}
    for i, j in SIDES:
        parts = []
        if i:
            parts.append(gx > 0 if i < 0 else gx < nx - 1)
        if j:
            parts.append(gy > 0 if j < 0 else gy < ny - 1)
        has[i, j] = functools.reduce(jnp.logical_and, parts)

    def device(i, j):
        return (lax.rem(gx + i + nx, nx), lax.rem(gy + j + ny, ny))

    mirror = (nx - 1 - gx, gy)

    barrier = pltpu.get_barrier_semaphore()
    greeted = jnp.int32(1)
    for side in SIDES:
        greeted = greeted + has[side].astype(jnp.int32)

        @pl.when(has[side])
        def _():
            pl.semaphore_signal(barrier, inc=1, device_id=device(*side), device_id_type=MESH)

    pl.semaphore_signal(barrier, inc=1, device_id=mirror, device_id_type=MESH)

    loads = [
        pltpu.make_async_copy(src, dst, in_sems.at[k])
        for k, (src, dst) in enumerate(
            [
                (electric_in, v_electric),
                (magnetic_in, v_magnetic),
                (polar_in, v_polar),
                (rate_in, v_rate),
                (density_in, v_density),
                (forward_in, v_forward),
                (mask_in, v_mask),
                (radius_in, v_radius),
                (partner_in, partner),
            ]
        )
    ]
    for load in loads:
        load.start()

    lane = lax.broadcasted_iota(jnp.int32, (rows_x, 128), 1)

    def ahead_z(v):
        return jnp.where(lane < 127, pltpu.roll(v, 127, 1), 0.0)

    def behind_z(v):
        return jnp.where(lane > 0, pltpu.roll(v, 1, 1), 0.0)

    def over_rows(body, stop=rows_y, start=0):
        def step(y, carry):
            body(y)
            return carry

        lax.fori_loop(start, stop, step, 0)

    zeros_slab = jnp.zeros((rows_x, 128), jnp.float32)
    zeros_edge = jnp.zeros((EDGE, 128), jnp.float32)
    for s in range(STEPS):
        for c in range(3):
            efield[s, c, own(rows_y), :] = zeros_slab

            def clear(y, s=s, c=c):
                efield[s, c, edge(y, EDGE + rows_x), :] = zeros_edge

            over_rows(clear)

    def native(ref, y):
        return ref[pl.ds(y, rows_x, stride=rows_y), :]

    loads[0].wait()

    def stage(y):
        for c in range(3):
            efield[0, c, own(y), :] = native(v_electric.at[ORDER[c]], y)

    over_rows(stage)
    loads[1].wait()

    distances = sorted({a * a + b * b for a in range(RMAX) for b in range(RMAX) if a * a + b * b < RMAX * RMAX})

    def filtered_sum(ref, emit):
        def pair(y):
            for a in range(1, RMAX):
                sums[a - 1, y] = (
                    ref[rows(y, EDGE + a), :] + ref[rows(y, EDGE - a), :]
                )

        over_rows(pair, rows_y + 2 * WIDTH)

        def gather(y):
            def column(a, b):
                if a == 0:
                    return ref[own(y + WIDTH + b), :]
                return sums[a - 1, y + WIDTH + b]

            by_distance = {}
            for a in range(RMAX):
                for b in range(RMAX):
                    d = a * a + b * b
                    if d not in distances:
                        continue
                    term = column(a, 0) if b == 0 else column(a, b) + column(a, -b)
                    by_distance[d] = by_distance[d] + term if d in by_distance else term
            radius = weight_radius[y]
            total = radius * by_distance[0]
            for d in distances[1:]:
                total = total + jnp.maximum(radius - math.sqrt(d), 0.0) * by_distance[d]
            emit(y, total)

        over_rows(gather)

    def settle():
        for s in range(STEPS):
            for refs, shape, side in (
                (ye_recv, zeros_slab, (0, 1)),
                (yh_recv, zeros_slab, (0, -1)),
                (xe_recv, zeros_edge, (1, 0)),
                (xh_recv, zeros_edge, (-1, 0)),
            ):

                @pl.when(jnp.logical_not(has[side]))
                def _():
                    for k in range(2):
                        refs[s, k] = shape

            for ref, side in ((d1_recv, (1, -1)), (d2_recv, (-1, 1))):

                @pl.when(jnp.logical_not(has[side]))
                def _():
                    ref[s] = zeros_edge

        def frame(ref, i, j):
            xs = {-1: (0, EDGE), 0: (EDGE, rows_x), 1: (EDGE + rows_x, EDGE)}[i]
            ys = {-1: range(WIDTH), 0: range(WIDTH, WIDTH + rows_y), 1: range(WIDTH + rows_y, 2 * WIDTH + rows_y)}[j]
            return xs, ys

        ones_slab = jnp.ones((rows_x, 128), jnp.float32)
        over_rows(lambda y: covered.__setitem__((own(y + WIDTH), slice(None)), ones_slab))
        for i, j in SIDES:
            xs, ys = frame(covered, i, j)
            inside = jnp.where(has[i, j], jnp.float32(1.0), jnp.float32(0.0))
            filler = jnp.zeros((xs[1], 128), jnp.float32) + inside
            for y in ys:
                covered[rows(y, *xs), :] = filler

        for k in range(2):
            for refs, side in ((xf_recv.at[k], (2 * k - 1, 0)), (yf_recv.at[k], (0, 2 * k - 1))):

                @pl.when(jnp.logical_not(has[side]))
                def _():
                    refs[...] = jnp.zeros(refs.shape, jnp.float32)

            for j in range(2):

                @pl.when(jnp.logical_not(has[2 * k - 1, 2 * j - 1]))
                def _():
                    cf_recv[k, j] = jnp.zeros((WIDTH, EDGE, 128), jnp.float32)

        loads[7].wait()
        radii = v_radius[...].astype(jnp.float32).T
        for y in range(rows_y):
            weight_radius[y] = jnp.broadcast_to(radii[:, y : y + 1], (rows_x, 128))

        filtered_sum(covered, lambda y, total: inv_denom.__setitem__(y, 1.0 / total))
        for load in loads[2:7] + loads[8:]:
            load.wait()

    def column_of(ref, x, first):
        return ref.at[pl.ds(first * slab + EDGE + x, rows_y, stride=slab), :]

    behind_mask_x = jnp.where(has[-1, 0], jnp.float32(COURANT), jnp.float32(0.0))
    behind_mask_y = jnp.where(has[0, -1], jnp.float32(COURANT), jnp.float32(0.0))

    def copies(s):
        base = 6 * s

        def copy(k, src, dst, side):
            return pltpu.make_async_remote_copy(
                src_ref=src,
                dst_ref=dst,
                send_sem=send_sems.at[base + k],
                recv_sem=recv_sems.at[base + k],
                device_id=device(*side),
                device_id_type=MESH,
            )

        return [
            ((0, -1), copy(2, efield.at[s, 0:2, own(0), :], ye_recv.at[s], (0, -1))),
            ((0, 1), copy(3, yh_send.at[s], yh_recv.at[s], (0, 1))),
            ((1, -1), copy(5, efield.at[s, 0, edge(0, rows_x), :], d2_recv.at[s], (1, -1))),
            ((-1, 0), copy(0, xe_send.at[s], xe_recv.at[s], (-1, 0))),
            ((1, 0), copy(1, xh_send.at[s], xh_recv.at[s], (1, 0))),
            ((-1, 1), copy(4, xe_send.at[s, 1], d1_recv.at[s], (-1, 1))),
        ]

    def start(pairs):
        for side, copy in pairs:
            pl.when(has[side])(copy.start)

    def arrive(pairs):
        for (i, j), copy in pairs:
            pl.when(has[-i, -j])(copy.wait_recv)

    def sent(pairs):
        for side, copy in pairs:
            pl.when(has[side])(copy.wait_send)

    def column(y):
        return pl.ds(y * rows_x if isinstance(y, int) else pl.multiple_of(y * rows_x, rows_x), rows_x)

    def curled(s, y):
        ex, ez, ey = (efield[s, c, own(y), :] for c in range(3))
        ex_y, ez_y = (efield[s, c, own(y + 1), :] for c in (0, 1))
        ez_x, ey_x = (efield[s, c, rows(y, EDGE + 1), :] for c in (1, 2))
        if s == 0:
            hx, hz, hy = (native(v_magnetic.at[ORDER[c]], y) for c in range(3))
        else:
            hx, hz, hy = (hfield[s - 1, c, own(y + 1), :] for c in range(3))
        hfield[s, 0, own(y + 1), :] = hx - COURANT * ((ez_y - ez) - (ahead_z(ey) - ey))
        hfield[s, 2, own(y + 1), :] = hy - COURANT * ((ahead_z(ex) - ex) - (ez_x - ez))
        hfield[s, 1, own(y + 1), :] = hz - COURANT * ((ey_x - ey) - (ex_y - ex))

    def driven_by(s, y, fields):
        material = (OMEGA_SQUARED * LORENTZ_STRENGTH) * native(v_density, y)
        scale = inv_eps[y]
        for c in range(3):
            if s == 0:
                p, q = native(v_polar.at[ORDER[c]], y), native(v_rate.at[ORDER[c]], y)
            else:
                p, q = polar[c, y], rate[c, y]
            q = DAMPING * q - OMEGA_SQUARED * p + material * fields[c]
            if s + 1 < STEPS:
                polar[c, y] = p + q
                rate[c, y] = q
            driven[c, y] = fields[c] - q * scale

    def advanced(s, y):
        hx, hz, hy = (hfield[s, c, own(y + 1), :] for c in range(3))
        hx_y, hz_y = (hfield[s, c, own(y), :] for c in (0, 1))
        hz_x, hy_x = (hfield[s, c, rows(y + 1, EDGE - 1), :] for c in (1, 2))
        curls = (
            (hz - hz_y) - (hy - behind_z(hy)),
            (hy - hy_x) - (hx - hx_y),
            (hx - behind_z(hx)) - (hz - hz_x),
        )
        scale = COURANT * inv_eps[y]
        news = [driven[c, y] + curls[c] * scale for c in range(3)]
        total = None
        for c in range(3):
            term = news[c] * native(v_forward.at[3 * s + ORDER[c]], y)
            total = term if total is None else total + term
        return (hx, hz, hy), news, total

    def flip(k, src, dst):
        return pltpu.make_async_remote_copy(
            src_ref=src,
            dst_ref=dst,
            send_sem=send_sems.at[k],
            recv_sem=recv_sems.at[k],
            device_id=mirror,
            device_id_type=MESH,
        )

    def inner_rows():
        def first(y):
            _, news, total = advanced(0, y)
            for c in range(3):
                efield[1, c, own(y), :] = news[c]
            gradient[column(y), :] = total

        over_rows(first, rows_y - 1, 1)
        over_rows(lambda y: curled(1, y), rows_y - 2, 1)

        def second(y):
            material = (OMEGA_SQUARED * LORENTZ_STRENGTH) * native(v_density, y)
            for c in range(3):
                kept[c, y] = driven[c, y]
                e = efield[1, c, own(y), :]
                q = DAMPING * rate[c, y] - OMEGA_SQUARED * polar[c, y] + material * e
                driven[c, y] = e - q * inv_eps[y]
            _, _, total = advanced(1, y)
            g_send[column(y), :] = gradient[column(y), :] + total
            for c in range(3):
                driven[c, y] = kept[c, y]

        over_rows(second, rows_y - 2, 2)

    inner = pl.ds(2 * rows_x, (rows_y - 4) * rows_x)
    flips = [flip(12, g_send.at[inner, :], g_recv.at[inner, :])]
    flips += [flip(13 + k, g_send.at[column(y), :], g_recv.at[column(y), :]) for k, y in enumerate((1, rows_y - 2))]
    flips += [flip(15 + k, gradient.at[column(y), :], g_recv.at[column(y), :]) for k, y in enumerate((0, rows_y - 1))]
    flips += [flip(17, ends_send, ends_recv)]
    ends = (0, 1, rows_x - 2, rows_x - 1)

    def whole(s, y):
        hs, news, total = advanced(s, y)
        for c in range(3):
            if s + 1 < STEPS:
                efield[s + 1, c, own(y), :] = news[c]
            else:
                o_electric[ORDER[c], pl.ds(y, rows_x, stride=rows_y), :] = news[c]
                o_magnetic[ORDER[c], pl.ds(y, rows_x, stride=rows_y), :] = hs[c]
        if s > 0:
            total = gradient[column(y), :] + total
        gradient[column(y), :] = total

    def faces_y(s):
        for k in range(2):
            yh_send[s, k] = hfield[s, k, own(rows_y), :]

    def faces_x(s):
        for k in range(2):
            xe_send[s, k] = column_of(efield.at[s, 1 + k], 0, 0)[...]
            xh_send[s, k] = column_of(hfield.at[s, 1 + k], rows_x - 1, 1)[...]

    pending = []
    for s in range(STEPS):

        pairs = copies(s)
        if s == 0:
            over_rows(lambda y: curled(0, y))
            faces_y(s)
            faces_x(s)
            pl.semaphore_wait(barrier, greeted)
            start(pairs)
        else:
            curled(s, rows_y - 1)
            faces_y(s)
            start(pairs[:3])
            over_rows(lambda y, s=s: whole(s - 1, y), rows_y - 1, 1)
            over_rows(lambda y, s=s: curled(s, y), rows_y - 1)
            faces_x(s)
            start(pairs[3:])
        if s == 0:
            settle()
            over_rows(
                lambda y: inv_eps.__setitem__(
                    y, 1.0 / (1.0 + (EPS_MATERIAL - 1.0) * native(v_density, y))
                )
            )

        def drive(y, s=s):
            driven_by(s, y, [efield[s, c, own(y), :] for c in range(3)])

        over_rows(drive)
        if s == 0:
            inner_rows()
            flips[0].start()
        else:
            for y in (1, rows_y - 2):
                g_send[column(y), :] = gradient[column(y), :] + advanced(s, y)[2]
            flips[1].start()
            flips[2].start()
        arrive(pairs)
        pending += pairs

        hfield[s, 0, own(rows_y), :] = hfield[s, 0, own(rows_y), :] - COURANT * ye_recv[s, 1]
        hfield[s, 1, own(rows_y), :] = hfield[s, 1, own(rows_y), :] + COURANT * ye_recv[s, 0]
        last_z = column_of(hfield.at[s, 1], rows_x - 1, 1)
        last_y = column_of(hfield.at[s, 2], rows_x - 1, 1)
        last_z[...] = last_z[...] - COURANT * xe_recv[s, 1]
        last_y[...] = last_y[...] + COURANT * xe_recv[s, 0]
        hfield[s, 0, own(0), :] = yh_recv[s, 0] - behind_mask_y * efield[s, 1, own(0), :]
        hfield[s, 1, own(0), :] = yh_recv[s, 1] + behind_mask_y * efield[s, 0, own(0), :]
        corner = hfield[s, 1, rows(0, EDGE + rows_x - 1, 1), :]
        hfield[s, 1, rows(0, EDGE + rows_x - 1, 1), :] = corner - COURANT * d1_recv[s, rows_y - 1 : rows_y, :]
        row = lax.broadcasted_iota(jnp.int32, (rows_y, 128), 0)
        extra = jnp.where(row == rows_y - 1, d2_recv[s, EDGE - 1 : EDGE, :], 0.0)
        column_of(hfield.at[s, 1], -1, 1)[...] = xh_recv[s, 0] - behind_mask_x * xe_send[s, 1] + COURANT * extra
        column_of(hfield.at[s, 2], -1, 1)[...] = xh_recv[s, 1] + behind_mask_x * xe_send[s, 0]

        over_rows(lambda k, s=s: whole(s, k * (rows_y - 1)), 2)

    for copy in flips[3:5]:
        copy.start()
    over_rows(lambda y: whole(STEPS - 1, y), rows_y - 1, 1)
    for k, x in enumerate(ends):
        ends_send[k] = gradient[pl.ds(x, rows_y, stride=rows_x), :]
    flips[5].start()
    for copy in flips:
        copy.wait_recv()

    def spread(y):
        g_turn[pl.ds(y, rows_x, stride=rows_y), :] = g_recv[column(y), :]

    over_rows(spread)
    for k, x in enumerate(ends):
        g_turn[pl.ds(x * rows_y, rows_y), :] = ends_recv[k]

    def turn(x):
        g_flip[pl.ds(pl.multiple_of(x * rows_y, rows_y), rows_y), :] = g_turn[
            pl.ds(pl.multiple_of((rows_x - 1 - x) * rows_y, rows_y), rows_y), :
        ]

    over_rows(turn, rows_x)

    def update(y):
        mirrored = g_flip[pl.ds(partner[y], rows_x, stride=rows_y), :]
        symmetric = 0.5 * (gradient[column(y), :] + mirrored)
        design = native(v_mask, y).astype(jnp.float32)
        updated[own(y + WIDTH), :] = native(v_density, y) - UPDATE_STEP * design * symmetric

    over_rows(update)

    for r in range(WIDTH):
        xf_send[0, r] = column_of(updated, r, WIDTH)[...]
        xf_send[1, r] = column_of(updated, rows_x - WIDTH + r, WIDTH)[...]
        yf_send[0, r] = updated[own(WIDTH + r), :]
        yf_send[1, r] = updated[own(rows_y + r), :]

    halos = []
    for k, (i, j) in enumerate(SIDES):
        if j == 0:
            src, dst = xf_send.at[(i + 1) // 2], xf_recv.at[(1 - i) // 2]
        elif i == 0:
            src, dst = yf_send.at[(j + 1) // 2], yf_recv.at[(1 - j) // 2]
        else:
            xs = slice(0, EDGE) if i < 0 else slice(rows_x - EDGE, rows_x)
            src, dst = yf_send.at[(j + 1) // 2, :, xs, :], cf_recv.at[(1 - i) // 2, (1 - j) // 2]
        halos.append(
            (
                (i, j),
                pltpu.make_async_remote_copy(
                    src_ref=src,
                    dst_ref=dst,
                    send_sem=send_sems.at[18 + k],
                    recv_sem=recv_sems.at[18 + k],
                    device_id=device(i, j),
                    device_id_type=MESH,
                ),
            )
        )
    start(halos)
    arrive(halos)
    for r in range(WIDTH):
        column_of(updated, r - WIDTH, WIDTH)[...] = xf_recv[0, r]
        column_of(updated, rows_x + r, WIDTH)[...] = xf_recv[1, r]
        for j in range(2):
            y = r + j * (WIDTH + rows_y)
            updated[own(y), :] = yf_recv[j, r]
            updated[edge(y, 0), :] = cf_recv[0, j, r]
            updated[edge(y, EDGE + rows_x), :] = cf_recv[1, j, r]

    top = math.tanh(SHARPNESS * THRESHOLD)
    bottom = top + math.tanh(SHARPNESS * (1.0 - THRESHOLD))

    def project(y, total):
        filtered = total * inv_denom[y]
        o_density[pl.ds(y, rows_x, stride=rows_y), :] = (
            top + jnp.tanh(SHARPNESS * (filtered - THRESHOLD))
        ) / bottom

    filtered_sum(updated, project)
    sent(pending)
    for copy in flips:
        copy.wait_send()
    sent(halos)


def write_out(electric, magnetic, density, electric_out, magnetic_out, density_out, sems):
    pairs = ((electric, electric_out), (magnetic, magnetic_out), (density, density_out))
    stores = [pltpu.make_async_copy(src, dst, sems.at[k]) for k, (src, dst) in enumerate(pairs)]
    for store in stores:
        store.start()
    for store in stores:
        store.wait()


def local(nx, ny, *args):
    rows_x, rows_y, depth = args[4].shape
    cells = rows_x * rows_y
    slab = rows_x + 2 * EDGE
    f32 = jnp.float32

    def vmem(*shape, dtype=f32):
        return pltpu.VMEM(shape, dtype)

    any_spec = pl.BlockSpec(memory_space=pl.ANY)
    electric, magnetic, polar, rate, density, forward, mask, partners, radius = args
    operands = (
        electric.reshape(3, cells, depth),
        magnetic.reshape(3, cells, depth),
        polar.reshape(3, cells, depth),
        rate.reshape(3, cells, depth),
        density.reshape(cells, depth),
        forward.reshape(3 * STEPS, cells, depth),
        mask.reshape(cells, depth),
        partners,
        radius.T,
    )
    in_specs = [any_spec] * 9
    shapes = ((3, cells, depth), (3, cells, depth), (cells, depth))
    vmem_spec = pl.BlockSpec(memory_space=pltpu.VMEM)
    held = pl.pallas_call(
        functools.partial(kernel, nx, ny),
        out_shape=tuple(pltpu.VMEM(shape, f32) for shape in shapes),
        in_specs=in_specs,
        out_specs=(vmem_spec,) * 3,
        scratch_shapes=[
            vmem(3, cells, depth),
            vmem(3, cells, depth),
            vmem(3, cells, depth),
            vmem(3, cells, depth),
            vmem(cells, depth),
            vmem(3 * STEPS, cells, depth),
            vmem(cells, depth, dtype=jnp.int32),
            vmem(rows_y, rows_x, dtype=jnp.int32),
            pltpu.SMEM((rows_y,), jnp.int32),
            vmem(STEPS, 3, (rows_y + 1) * slab, depth),
            vmem(STEPS, 3, (rows_y + 1) * slab, depth),
            vmem(3, rows_y, rows_x, depth),
            vmem(3, rows_y, rows_x, depth),
            vmem(3, rows_y, rows_x, depth),
            vmem(3, rows_y, rows_x, depth),
            vmem(rows_y, rows_x, depth),
            vmem(cells, depth),
            vmem(cells, depth),
            vmem(cells, depth),
            vmem(cells, depth),
            vmem(cells, depth),
            vmem(4, rows_y, depth),
            vmem(4, rows_y, depth),
            vmem((rows_y + 2 * WIDTH) * slab, depth),
            vmem((rows_y + 2 * WIDTH) * slab, depth),
            vmem(WIDTH, rows_y + 2 * WIDTH, rows_x, depth),
            vmem(rows_y, rows_x, depth),
            vmem(rows_y, rows_x, depth),
            vmem(STEPS, 2, rows_x, depth),
            vmem(STEPS, 2, rows_x, depth),
            vmem(STEPS, 2, rows_x, depth),
            vmem(STEPS, 2, rows_y, depth),
            vmem(STEPS, 2, rows_y, depth),
            vmem(STEPS, 2, rows_y, depth),
            vmem(STEPS, 2, rows_y, depth),
            vmem(STEPS, EDGE, depth),
            vmem(STEPS, EDGE, depth),
            vmem(2, WIDTH, rows_y, depth),
            vmem(2, WIDTH, rows_y, depth),
            vmem(2, WIDTH, rows_x, depth),
            vmem(2, WIDTH, rows_x, depth),
            vmem(2, 2, WIDTH, EDGE, depth),
            pltpu.SemaphoreType.DMA((9,)),
            pltpu.SemaphoreType.DMA((26,)),
            pltpu.SemaphoreType.DMA((26,)),
        ],
        compiler_params=pltpu.CompilerParams(collective_id=0, has_side_effects=True),
    )(*operands)
    outs = pl.pallas_call(
        write_out,
        out_shape=tuple(jax.ShapeDtypeStruct(shape, f32) for shape in shapes),
        in_specs=[vmem_spec] * 3,
        out_specs=(any_spec,) * 3,
        scratch_shapes=[pltpu.SemaphoreType.DMA((3,))],
    )(*[pltpu.with_memory_space_constraint(a, pltpu.VMEM) for a in held])
    return (
        outs[0].reshape(electric.shape),
        outs[1].reshape(magnetic.shape),
        outs[2].reshape(density.shape),
    )


def solution(mesh):
    in_specs = (
        P(None, "gx", "gy", None),
        P(None, "gx", "gy", None),
        P(None, "gx", "gy", None),
        P(None, "gx", "gy", None),
        P("gx", "gy", None),
        P(None, None, "gx", "gy", None),
        P("gx", "gy", None),
        P("gy"),
        P("gx", "gy"),
    )
    out_specs = (P(None, "gx", "gy", None), P(None, "gx", "gy", None), P("gx", "gy", None))
    return jax.shard_map(
        functools.partial(local, mesh.shape["gx"], mesh.shape["gy"]),
        mesh=mesh,
        in_specs=in_specs,
        out_specs=out_specs,
        check_vma=False,
    )
```

```python
import functools
import math

import jax
import jax.numpy as jnp
from jax import lax
from jax.experimental import pallas as pl
from jax.experimental.pallas import tpu as pltpu
from jax.sharding import PartitionSpec as P

STEPS = 2
RMAX = 4
COURANT = 0.5
DAMPING = 0.9
OMEGA_SQUARED = 0.3
LORENTZ_STRENGTH = 2.0
EPS_MATERIAL = 4.0
UPDATE_STEP = 0.25
SHARPNESS = 4.0
THRESHOLD = 0.5

MESH = pl.DeviceIdType.MESH
WIDTH = RMAX - 1
EDGE = 8
ORDER = (0, 2, 1)
SIDES = tuple((i, j) for i in (-1, 0, 1) for j in (-1, 0, 1) if (i, j) != (0, 0))


def kernel(
    nx,
    ny,
    electric_in,
    magnetic_in,
    polar_in,
    rate_in,
    density_in,
    forward_in,
    mask_in,
    partner_in,
    radius_in,
    o_electric,
    o_magnetic,
    o_density,
    v_electric,
    v_magnetic,
    v_polar,
    v_rate,
    v_density,
    v_forward,
    v_mask,
    v_radius,
    partner,
    efield,
    hfield,
    polar,
    rate,
    driven,
    kept,
    inv_eps,
    gradient,
    g_send,
    g_recv,
    g_turn,
    g_near,
    g_flip,
    ends_send,
    ends_recv,
    updated,
    covered,
    sums,
    weight_radius,
    inv_denom,
    ye_recv,
    yh_send,
    yh_recv,
    xe_send,
    xe_recv,
    xh_send,
    xh_recv,
    d1_recv,
    d2_recv,
    xf_send,
    xf_recv,
    yf_send,
    yf_recv,
    cf_recv,
    in_sems,
    send_sems,
    recv_sems,
):
    rows_y, rows_x = v_radius.shape
    slab = rows_x + 2 * EDGE

    def rows(y, first=EDGE, count=rows_x):
        return pl.ds(y * slab + first, count)

    def own(y):
        start = y * slab + EDGE
        return pl.ds(start if isinstance(start, int) else pl.multiple_of(start, EDGE), rows_x)

    def edge(y, first):
        start = y * slab + first
        return pl.ds(start if isinstance(start, int) else pl.multiple_of(start, EDGE), EDGE)

    gx, gy = lax.axis_index("gx"), lax.axis_index("gy")
    has = {}
    for i, j in SIDES:
        parts = []
        if i:
            parts.append(gx > 0 if i < 0 else gx < nx - 1)
        if j:
            parts.append(gy > 0 if j < 0 else gy < ny - 1)
        has[i, j] = functools.reduce(jnp.logical_and, parts)

    def device(i, j):
        return (lax.rem(gx + i + nx, nx), lax.rem(gy + j + ny, ny))

    mirror = (nx - 1 - gx, gy)

    barrier = pltpu.get_barrier_semaphore()
    pl.semaphore_signal(barrier, inc=1, device_id=mirror, device_id_type=MESH)
    greeted = jnp.int32(1)
    for side in sorted(SIDES, key=lambda p: (abs(p[0]), -abs(p[1]))):
        greeted = greeted + has[side].astype(jnp.int32)

        @pl.when(has[side])
        def _():
            pl.semaphore_signal(barrier, inc=1, device_id=device(*side), device_id_type=MESH)


    loads = [
        pltpu.make_async_copy(src, dst, in_sems.at[k])
        for k, (src, dst) in enumerate(
            [
                (electric_in, v_electric),
                (magnetic_in, v_magnetic),
                (polar_in, v_polar),
                (rate_in, v_rate),
                (density_in, v_density),
                (forward_in, v_forward),
                (mask_in, v_mask),
                (radius_in, v_radius),
                (partner_in, partner),
            ]
        )
    ]
    loads[0].start()
    loads[1].start()

    lane = lax.broadcasted_iota(jnp.int32, (rows_x, 128), 1)

    def ahead_z(v):
        return jnp.where(lane < 127, pltpu.roll(v, 127, 1), 0.0)

    def behind_z(v):
        return jnp.where(lane > 0, pltpu.roll(v, 1, 1), 0.0)

    def over_rows(body, stop=rows_y, start=0):
        def step(y, carry):
            body(y)
            return carry

        lax.fori_loop(start, stop, step, 0)

    zeros_slab = jnp.zeros((rows_x, 128), jnp.float32)
    zeros_edge = jnp.zeros((EDGE, 128), jnp.float32)
    for s in range(STEPS):
        for c in range(3):
            efield[s, c, own(rows_y), :] = zeros_slab

            def clear(y, s=s, c=c):
                efield[s, c, edge(y, EDGE + rows_x), :] = zeros_edge

            over_rows(clear)

    def native(ref, y):
        return ref[pl.ds(y, rows_x, stride=rows_y), :]

    loads[0].wait()
    for load in loads[2:]:
        load.start()

    def stage(y):
        for c in range(3):
            efield[0, c, own(y), :] = native(v_electric.at[ORDER[c]], y)

    over_rows(stage)
    loads[1].wait()

    distances = sorted({a * a + b * b for a in range(RMAX) for b in range(RMAX) if a * a + b * b < RMAX * RMAX})

    def filtered_sum(ref, emit):
        def pair(y):
            for a in range(1, RMAX):
                sums[a - 1, y] = (
                    ref[rows(y, EDGE + a), :] + ref[rows(y, EDGE - a), :]
                )

        over_rows(pair, rows_y + 2 * WIDTH)

        def gather(y):
            def column(a, b):
                if a == 0:
                    return ref[own(y + WIDTH + b), :]
                return sums[a - 1, y + WIDTH + b]

            by_distance = {}
            for a in range(RMAX):
                for b in range(RMAX):
                    d = a * a + b * b
                    if d not in distances:
                        continue
                    term = column(a, 0) if b == 0 else column(a, b) + column(a, -b)
                    by_distance[d] = by_distance[d] + term if d in by_distance else term
            radius = weight_radius[y]
            total = radius * by_distance[0]
            for d in distances[1:]:
                total = total + jnp.maximum(radius - math.sqrt(d), 0.0) * by_distance[d]
            emit(y, total)

        over_rows(gather)

    def settle():
        for s in range(STEPS):
            for refs, shape, side in (
                (ye_recv, zeros_slab, (0, 1)),
                (yh_recv, zeros_slab, (0, -1)),
                (xe_recv, zeros_edge, (1, 0)),
                (xh_recv, zeros_edge, (-1, 0)),
            ):

                @pl.when(jnp.logical_not(has[side]))
                def _():
                    for k in range(2):
                        refs[s, k] = shape

            for ref, side in ((d1_recv, (1, -1)), (d2_recv, (-1, 1))):

                @pl.when(jnp.logical_not(has[side]))
                def _():
                    ref[s] = zeros_edge

        def frame(ref, i, j):
            xs = {-1: (0, EDGE), 0: (EDGE, rows_x), 1: (EDGE + rows_x, EDGE)}[i]
            ys = {-1: range(WIDTH), 0: range(WIDTH, WIDTH + rows_y), 1: range(WIDTH + rows_y, 2 * WIDTH + rows_y)}[j]
            return xs, ys

        ones_slab = jnp.ones((rows_x, 128), jnp.float32)
        over_rows(lambda y: covered.__setitem__((own(y + WIDTH), slice(None)), ones_slab))
        for i, j in SIDES:
            xs, ys = frame(covered, i, j)
            inside = jnp.where(has[i, j], jnp.float32(1.0), jnp.float32(0.0))
            filler = jnp.zeros((xs[1], 128), jnp.float32) + inside
            for y in ys:
                covered[rows(y, *xs), :] = filler

        for k in range(2):
            for refs, side in ((xf_recv.at[k], (2 * k - 1, 0)), (yf_recv.at[k], (0, 2 * k - 1))):

                @pl.when(jnp.logical_not(has[side]))
                def _():
                    refs[...] = jnp.zeros(refs.shape, jnp.float32)

            for j in range(2):

                @pl.when(jnp.logical_not(has[2 * k - 1, 2 * j - 1]))
                def _():
                    cf_recv[k, j] = jnp.zeros((WIDTH, WIDTH, 128), jnp.float32)

        loads[7].wait()
        radii = v_radius[...].astype(jnp.float32).T
        for y in range(rows_y):
            weight_radius[y] = jnp.broadcast_to(radii[:, y : y + 1], (rows_x, 128))

        filtered_sum(covered, lambda y, total: inv_denom.__setitem__(y, 1.0 / total))

    def column_of(ref, x, first):
        return ref.at[pl.ds(first * slab + EDGE + x, rows_y, stride=slab), :]

    behind_mask_x = jnp.where(has[-1, 0], jnp.float32(COURANT), jnp.float32(0.0))
    behind_mask_y = jnp.where(has[0, -1], jnp.float32(COURANT), jnp.float32(0.0))

    def copies(s):
        base = 6 * s

        def copy(k, src, dst, side):
            return pltpu.make_async_remote_copy(
                src_ref=src,
                dst_ref=dst,
                send_sem=send_sems.at[base + k],
                recv_sem=recv_sems.at[base + k],
                device_id=device(*side),
                device_id_type=MESH,
            )

        return [
            ((0, -1), copy(2, efield.at[s, 0:2, own(0), :], ye_recv.at[s], (0, -1))),
            ((0, 1), copy(3, yh_send.at[s], yh_recv.at[s], (0, 1))),
            ((1, -1), copy(5, efield.at[s, 0, edge(0, rows_x), :], d2_recv.at[s], (1, -1))),
            ((-1, 0), copy(0, xe_send.at[s], xe_recv.at[s], (-1, 0))),
            ((1, 0), copy(1, xh_send.at[s], xh_recv.at[s], (1, 0))),
            ((-1, 1), copy(4, xe_send.at[s, 1], d1_recv.at[s], (-1, 1))),
        ]

    def start(pairs):
        for side, copy in pairs:
            pl.when(has[side])(copy.start)

    def arrive(pairs):
        for (i, j), copy in pairs:
            pl.when(has[-i, -j])(copy.wait_recv)

    def sent(pairs):
        for side, copy in pairs:
            pl.when(has[side])(copy.wait_send)

    def column(y):
        return pl.ds(y * rows_x if isinstance(y, int) else pl.multiple_of(y * rows_x, rows_x), rows_x)

    def curled(s, y):
        ex, ez, ey = (efield[s, c, own(y), :] for c in range(3))
        ex_y, ez_y = (efield[s, c, own(y + 1), :] for c in (0, 1))
        ez_x, ey_x = (efield[s, c, rows(y, EDGE + 1), :] for c in (1, 2))
        if s == 0:
            hx, hz, hy = (native(v_magnetic.at[ORDER[c]], y) for c in range(3))
        else:
            hx, hz, hy = (hfield[s - 1, c, own(y + 1), :] for c in range(3))
        hfield[s, 0, own(y + 1), :] = hx - COURANT * ((ez_y - ez) - (ahead_z(ey) - ey))
        hfield[s, 2, own(y + 1), :] = hy - COURANT * ((ahead_z(ex) - ex) - (ez_x - ez))
        hfield[s, 1, own(y + 1), :] = hz - COURANT * ((ey_x - ey) - (ex_y - ex))

    def driven_by(s, y, fields):
        material = (OMEGA_SQUARED * LORENTZ_STRENGTH) * native(v_density, y)
        scale = inv_eps[y]
        for c in range(3):
            if s == 0:
                p, q = native(v_polar.at[ORDER[c]], y), native(v_rate.at[ORDER[c]], y)
            else:
                p, q = polar[c, y], rate[c, y]
            q = DAMPING * q - OMEGA_SQUARED * p + material * fields[c]
            if s + 1 < STEPS:
                polar[c, y] = p + q
                rate[c, y] = q
            driven[c, y] = fields[c] - q * scale

    def advanced(s, y):
        hx, hz, hy = (hfield[s, c, own(y + 1), :] for c in range(3))
        hx_y, hz_y = (hfield[s, c, own(y), :] for c in (0, 1))
        hz_x, hy_x = (hfield[s, c, rows(y + 1, EDGE - 1), :] for c in (1, 2))
        curls = (
            (hz - hz_y) - (hy - behind_z(hy)),
            (hy - hy_x) - (hx - hx_y),
            (hx - behind_z(hx)) - (hz - hz_x),
        )
        scale = COURANT * inv_eps[y]
        news = [driven[c, y] + curls[c] * scale for c in range(3)]
        total = None
        for c in range(3):
            term = news[c] * native(v_forward.at[3 * s + ORDER[c]], y)
            total = term if total is None else total + term
        return (hx, hz, hy), news, total

    def flip(k, src, dst):
        return pltpu.make_async_remote_copy(
            src_ref=src,
            dst_ref=dst,
            send_sem=send_sems.at[k],
            recv_sem=recv_sems.at[k],
            device_id=mirror,
            device_id_type=MESH,
        )

    def inner_rows():
        def first(y):
            _, news, total = advanced(0, y)
            for c in range(3):
                efield[1, c, own(y), :] = news[c]
            gradient[column(y), :] = total

        over_rows(first, rows_y - 1, 1)
        over_rows(lambda y: curled(1, y), rows_y - 2, 1)

        def second(y):
            material = (OMEGA_SQUARED * LORENTZ_STRENGTH) * native(v_density, y)
            for c in range(3):
                kept[c, y] = driven[c, y]
                e = efield[1, c, own(y), :]
                q = DAMPING * rate[c, y] - OMEGA_SQUARED * polar[c, y] + material * e
                driven[c, y] = e - q * inv_eps[y]
            _, _, total = advanced(1, y)
            g_send[column(y), :] = gradient[column(y), :] + total
            for c in range(3):
                driven[c, y] = kept[c, y]

        over_rows(second, rows_y - 2, 2)

    inner = pl.ds(2 * rows_x, (rows_y - 4) * rows_x)
    flips = [flip(12, g_send.at[inner, :], g_recv.at[inner, :])]
    flips += [flip(13 + k, g_near.at[column(y), :], g_recv.at[column(y), :]) for k, y in enumerate((1, rows_y - 2))]
    flips += [flip(15 + k, gradient.at[column(y), :], g_recv.at[column(y), :]) for k, y in enumerate((0, rows_y - 1))]
    flips += [flip(17 + 9 * k, ends_send.at[pl.ds(2 * (1 - k), 2)], ends_recv.at[pl.ds(2 * (1 - k), 2)]) for k in range(2)]
    ends = (1, rows_x - 2, 0, rows_x - 1)

    def whole(s, y):
        hs, news, total = advanced(s, y)
        for c in range(3):
            if s + 1 < STEPS:
                efield[s + 1, c, own(y), :] = news[c]
            else:
                o_electric[ORDER[c], pl.ds(y, rows_x, stride=rows_y), :] = news[c]
                o_magnetic[ORDER[c], pl.ds(y, rows_x, stride=rows_y), :] = hs[c]
        if s > 0:
            total = gradient[column(y), :] + total
        gradient[column(y), :] = total

    def faces_y(s):
        for k in range(2):
            yh_send[s, k] = hfield[s, k, own(rows_y), :]

    def faces_x(s):
        for k in range(2):
            xe_send[s, k] = column_of(efield.at[s, 1 + k], 0, 0)[...]
            xh_send[s, k] = column_of(hfield.at[s, 1 + k], rows_x - 1, 1)[...]

    def drive(s, y):
        driven_by(s, y, [efield[s, c, own(y), :] for c in range(3)])

    def prepare():
        for load in loads[2:7] + loads[8:]:
            load.wait()
        over_rows(
            lambda y: inv_eps.__setitem__(y, 1.0 / (1.0 + (EPS_MATERIAL - 1.0) * native(v_density, y)))
        )
        over_rows(lambda y: drive(0, y))
        inner_rows()

    pending = []
    for s in range(STEPS):

        pairs = copies(s)
        if s == 0:
            over_rows(lambda y: curled(0, y))
            faces_y(s)
            faces_x(s)
            pl.semaphore_wait(barrier, greeted)
            start(pairs)
        else:
            curled(s, rows_y - 1)
            faces_y(s)
            start(pairs[:3])
            over_rows(lambda y, s=s: whole(s - 1, y), rows_y - 1, 1)
            over_rows(lambda y, s=s: curled(s, y), rows_y - 1)
            faces_x(s)
            start(pairs[3:])
        if s == 0:
            prepare()
            flips[0].start()
            settle()
        else:
            over_rows(lambda y, s=s: drive(s, y))

            def near(y):
                g_near[column(y), :] = gradient[column(y), :] + advanced(STEPS - 1, y)[2]

            over_rows(near, rows_y - 1, 1)
            for k, x in enumerate((1, rows_x - 2)):
                ends_send[k] = g_near[pl.ds(x, rows_y, stride=rows_x), :]
            for copy in flips[1:3] + flips[6:]:
                copy.start()
        arrive(pairs)
        pending += pairs

        hfield[s, 0, own(rows_y), :] = hfield[s, 0, own(rows_y), :] - COURANT * ye_recv[s, 1]
        hfield[s, 1, own(rows_y), :] = hfield[s, 1, own(rows_y), :] + COURANT * ye_recv[s, 0]
        last_z = column_of(hfield.at[s, 1], rows_x - 1, 1)
        last_y = column_of(hfield.at[s, 2], rows_x - 1, 1)
        last_z[...] = last_z[...] - COURANT * xe_recv[s, 1]
        last_y[...] = last_y[...] + COURANT * xe_recv[s, 0]
        hfield[s, 0, own(0), :] = yh_recv[s, 0] - behind_mask_y * efield[s, 1, own(0), :]
        hfield[s, 1, own(0), :] = yh_recv[s, 1] + behind_mask_y * efield[s, 0, own(0), :]
        corner = hfield[s, 1, rows(0, EDGE + rows_x - 1, 1), :]
        hfield[s, 1, rows(0, EDGE + rows_x - 1, 1), :] = corner - COURANT * d1_recv[s, rows_y - 1 : rows_y, :]
        row = lax.broadcasted_iota(jnp.int32, (rows_y, 128), 0)
        extra = jnp.where(row == rows_y - 1, d2_recv[s, EDGE - 1 : EDGE, :], 0.0)
        column_of(hfield.at[s, 1], -1, 1)[...] = xh_recv[s, 0] - behind_mask_x * xe_send[s, 1] + COURANT * extra
        column_of(hfield.at[s, 2], -1, 1)[...] = xh_recv[s, 1] + behind_mask_x * xe_send[s, 0]

        over_rows(lambda k, s=s: whole(s, k * (rows_y - 1)), 2)

    for copy in flips[3:5]:
        copy.start()
    over_rows(lambda y: whole(STEPS - 1, y), rows_y - 1, 1)
    for k, x in enumerate((0, rows_x - 1)):
        ends_send[2 + k] = gradient[pl.ds(x, rows_y, stride=rows_x), :]
    flips[5].start()
    for copy in flips:
        copy.wait_recv()

    def spread(ref, y):
        g_turn[pl.ds(y, rows_x, stride=rows_y), :] = ref[column(y), :]

    over_rows(lambda y: spread(g_recv, y))
    for k, x in enumerate(ends):
        g_turn[pl.ds(x * rows_y, rows_y), :] = ends_recv[k]
    for y in (0, rows_y - 1):
        spread(g_recv, y)

    def turn(x):
        g_flip[pl.ds(pl.multiple_of(x * rows_y, rows_y), rows_y), :] = g_turn[
            pl.ds(pl.multiple_of((rows_x - 1 - x) * rows_y, rows_y), rows_y), :
        ]

    over_rows(turn, rows_x)

    def update(y):
        mirrored = g_flip[pl.ds(partner[y], rows_x, stride=rows_y), :]
        symmetric = 0.5 * (gradient[column(y), :] + mirrored)
        design = native(v_mask, y).astype(jnp.float32)
        updated[own(y + WIDTH), :] = native(v_density, y) - UPDATE_STEP * design * symmetric

    over_rows(update)

    for r in range(WIDTH):
        xf_send[0, r] = column_of(updated, r, WIDTH)[...]
        xf_send[1, r] = column_of(updated, rows_x - WIDTH + r, WIDTH)[...]
        yf_send[0, r] = updated[own(WIDTH + r), :]
        yf_send[1, r] = updated[own(rows_y + r), :]

    halos = []
    for k, (i, j) in enumerate(SIDES):
        if j == 0:
            src, dst = xf_send.at[(i + 1) // 2], xf_recv.at[(1 - i) // 2]
        elif i == 0:
            src, dst = yf_send.at[(j + 1) // 2], yf_recv.at[(1 - j) // 2]
        else:
            xs = slice(0, WIDTH) if i < 0 else slice(rows_x - WIDTH, rows_x)
            src, dst = yf_send.at[(j + 1) // 2, :, xs, :], cf_recv.at[(1 - i) // 2, (1 - j) // 2]
        halos.append(
            (
                (i, j),
                pltpu.make_async_remote_copy(
                    src_ref=src,
                    dst_ref=dst,
                    send_sem=send_sems.at[18 + k],
                    recv_sem=recv_sems.at[18 + k],
                    device_id=device(i, j),
                    device_id_type=MESH,
                ),
            )
        )
    start(halos)
    arrive(halos)
    for r in range(WIDTH):
        column_of(updated, r - WIDTH, WIDTH)[...] = xf_recv[0, r]
        column_of(updated, rows_x + r, WIDTH)[...] = xf_recv[1, r]
        for j in range(2):
            y = r + j * (WIDTH + rows_y)
            updated[own(y), :] = yf_recv[j, r]
            updated[rows(y, EDGE - WIDTH, WIDTH), :] = cf_recv[0, j, r]
            updated[rows(y, EDGE + rows_x, WIDTH), :] = cf_recv[1, j, r]

    top = math.tanh(SHARPNESS * THRESHOLD)
    bottom = top + math.tanh(SHARPNESS * (1.0 - THRESHOLD))

    def project(y, total):
        filtered = total * inv_denom[y]
        o_density[pl.ds(y, rows_x, stride=rows_y), :] = (
            top + jnp.tanh(SHARPNESS * (filtered - THRESHOLD))
        ) / bottom

    filtered_sum(updated, project)
    sent(pending)
    for copy in flips:
        copy.wait_send()
    sent(halos)


def write_out(electric, magnetic, density, electric_out, magnetic_out, density_out, sems):
    pairs = ((electric, electric_out), (magnetic, magnetic_out), (density, density_out))
    pairs = [(src.at[c], dst.at[c]) for src, dst in pairs[:2] for c in range(3)] + [pairs[2]]
    stores = [pltpu.make_async_copy(src, dst, sems.at[k]) for k, (src, dst) in enumerate(pairs)]
    for store in stores:
        store.start()
    for store in stores:
        store.wait()


def local(nx, ny, *args):
    rows_x, rows_y, depth = args[4].shape
    cells = rows_x * rows_y
    slab = rows_x + 2 * EDGE
    f32 = jnp.float32

    def vmem(*shape, dtype=f32):
        return pltpu.VMEM(shape, dtype)

    any_spec = pl.BlockSpec(memory_space=pl.ANY)
    electric, magnetic, polar, rate, density, forward, mask, partners, radius = args
    operands = (
        electric.reshape(3, cells, depth),
        magnetic.reshape(3, cells, depth),
        polar.reshape(3, cells, depth),
        rate.reshape(3, cells, depth),
        density.reshape(cells, depth),
        forward.reshape(3 * STEPS, cells, depth),
        mask.reshape(cells, depth),
        partners,
        radius.T,
    )
    in_specs = [any_spec] * 9
    shapes = ((3, cells, depth), (3, cells, depth), (cells, depth))
    vmem_spec = pl.BlockSpec(memory_space=pltpu.VMEM)
    held = pl.pallas_call(
        functools.partial(kernel, nx, ny),
        out_shape=tuple(pltpu.VMEM(shape, f32) for shape in shapes),
        in_specs=in_specs,
        out_specs=(vmem_spec,) * 3,
        scratch_shapes=[
            vmem(3, cells, depth),
            vmem(3, cells, depth),
            vmem(3, cells, depth),
            vmem(3, cells, depth),
            vmem(cells, depth),
            vmem(3 * STEPS, cells, depth),
            vmem(cells, depth, dtype=jnp.int32),
            vmem(rows_y, rows_x, dtype=jnp.int32),
            pltpu.SMEM((rows_y,), jnp.int32),
            vmem(STEPS, 3, (rows_y + 1) * slab, depth),
            vmem(STEPS, 3, (rows_y + 1) * slab, depth),
            vmem(3, rows_y, rows_x, depth),
            vmem(3, rows_y, rows_x, depth),
            vmem(3, rows_y, rows_x, depth),
            vmem(3, rows_y, rows_x, depth),
            vmem(rows_y, rows_x, depth),
            vmem(cells, depth),
            vmem(cells, depth),
            vmem(cells, depth),
            vmem(cells, depth),
            vmem(cells, depth),
            vmem(cells, depth),
            vmem(4, rows_y, depth),
            vmem(4, rows_y, depth),
            vmem((rows_y + 2 * WIDTH) * slab, depth),
            vmem((rows_y + 2 * WIDTH) * slab, depth),
            vmem(WIDTH, rows_y + 2 * WIDTH, rows_x, depth),
            vmem(rows_y, rows_x, depth),
            vmem(rows_y, rows_x, depth),
            vmem(STEPS, 2, rows_x, depth),
            vmem(STEPS, 2, rows_x, depth),
            vmem(STEPS, 2, rows_x, depth),
            vmem(STEPS, 2, rows_y, depth),
            vmem(STEPS, 2, rows_y, depth),
            vmem(STEPS, 2, rows_y, depth),
            vmem(STEPS, 2, rows_y, depth),
            vmem(STEPS, EDGE, depth),
            vmem(STEPS, EDGE, depth),
            vmem(2, WIDTH, rows_y, depth),
            vmem(2, WIDTH, rows_y, depth),
            vmem(2, WIDTH, rows_x, depth),
            vmem(2, WIDTH, rows_x, depth),
            vmem(2, 2, WIDTH, WIDTH, depth),
            pltpu.SemaphoreType.DMA((9,)),
            pltpu.SemaphoreType.DMA((27,)),
            pltpu.SemaphoreType.DMA((27,)),
        ],
        compiler_params=pltpu.CompilerParams(collective_id=0, has_side_effects=True),
    )(*operands)
    outs = pl.pallas_call(
        write_out,
        out_shape=tuple(jax.ShapeDtypeStruct(shape, f32) for shape in shapes),
        in_specs=[vmem_spec] * 3,
        out_specs=(any_spec,) * 3,
        scratch_shapes=[pltpu.SemaphoreType.DMA((7,))],
    )(*[pltpu.with_memory_space_constraint(a, pltpu.VMEM) for a in held])
    return (
        outs[0].reshape(electric.shape),
        outs[1].reshape(magnetic.shape),
        outs[2].reshape(density.shape),
    )


def solution(mesh):
    in_specs = (
        P(None, "gx", "gy", None),
        P(None, "gx", "gy", None),
        P(None, "gx", "gy", None),
        P(None, "gx", "gy", None),
        P("gx", "gy", None),
        P(None, None, "gx", "gy", None),
        P("gx", "gy", None),
        P("gy"),
        P("gx", "gy"),
    )
    out_specs = (P(None, "gx", "gy", None), P(None, "gx", "gy", None), P("gx", "gy", None))
    return jax.shard_map(
        functools.partial(local, mesh.shape["gx"], mesh.shape["gy"]),
        mesh=mesh,
        in_specs=in_specs,
        out_specs=out_specs,
        check_vma=False,
    )
```

```python
import functools
import math

import jax
import jax.numpy as jnp
from jax import lax
from jax.experimental import pallas as pl
from jax.experimental.pallas import tpu as pltpu
from jax.sharding import PartitionSpec as P

STEPS = 2
RMAX = 4
COURANT = 0.5
DAMPING = 0.9
OMEGA_SQUARED = 0.3
LORENTZ_STRENGTH = 2.0
EPS_MATERIAL = 4.0
UPDATE_STEP = 0.25
SHARPNESS = 4.0
THRESHOLD = 0.5

MESH = pl.DeviceIdType.MESH
WIDTH = RMAX - 1
EDGE = 8
ORDER = (0, 2, 1)
SIDES = tuple((i, j) for i in (-1, 0, 1) for j in (-1, 0, 1) if (i, j) != (0, 0))


def kernel(
    nx,
    ny,
    electric_in,
    magnetic_in,
    polar_in,
    rate_in,
    density_in,
    forward_in,
    mask_in,
    partner_in,
    radius_in,
    o_electric,
    o_magnetic,
    o_density,
    v_electric,
    v_magnetic,
    v_polar,
    v_rate,
    v_density,
    v_forward,
    v_mask,
    v_radius,
    partner,
    efield,
    hfield,
    polar,
    rate,
    driven,
    kept,
    inv_eps,
    gradient,
    g_send,
    g_recv,
    g_turn,
    g_near,
    g_flip,
    ends_send,
    ends_recv,
    updated,
    covered,
    sums,
    weight_radius,
    inv_denom,
    ye_recv,
    yh_send,
    yh_recv,
    xe_send,
    xe_recv,
    xh_send,
    xh_recv,
    d1_recv,
    d2_recv,
    xf_send,
    xf_recv,
    yf_send,
    yf_recv,
    cf_recv,
    in_sems,
    send_sems,
    recv_sems,
):
    rows_y, rows_x = v_radius.shape
    slab = rows_x + 2 * EDGE

    def rows(y, first=EDGE, count=rows_x):
        return pl.ds(y * slab + first, count)

    def own(y):
        start = y * slab + EDGE
        return pl.ds(start if isinstance(start, int) else pl.multiple_of(start, EDGE), rows_x)

    def edge(y, first):
        start = y * slab + first
        return pl.ds(start if isinstance(start, int) else pl.multiple_of(start, EDGE), EDGE)

    gx, gy = lax.axis_index("gx"), lax.axis_index("gy")
    has = {}
    for i, j in SIDES:
        parts = []
        if i:
            parts.append(gx > 0 if i < 0 else gx < nx - 1)
        if j:
            parts.append(gy > 0 if j < 0 else gy < ny - 1)
        has[i, j] = functools.reduce(jnp.logical_and, parts)

    def device(i, j):
        return (lax.rem(gx + i + nx, nx), lax.rem(gy + j + ny, ny))

    mirror = (nx - 1 - gx, gy)

    barrier = pltpu.get_barrier_semaphore()
    pl.semaphore_signal(barrier, inc=1, device_id=mirror, device_id_type=MESH)
    greeted = jnp.int32(1)
    for side in sorted(SIDES, key=lambda p: (abs(p[0]), -abs(p[1]))):
        greeted = greeted + has[side].astype(jnp.int32)

        @pl.when(has[side])
        def _():
            pl.semaphore_signal(barrier, inc=1, device_id=device(*side), device_id_type=MESH)


    loads = [
        pltpu.make_async_copy(src, dst, in_sems.at[k])
        for k, (src, dst) in enumerate(
            [
                (electric_in, v_electric),
                (magnetic_in, v_magnetic),
                (polar_in, v_polar),
                (rate_in, v_rate),
                (density_in, v_density),
                (forward_in, v_forward),
                (mask_in, v_mask),
                (radius_in, v_radius),
                (partner_in, partner),
            ]
        )
    ]
    loads[0].start()
    loads[1].start()

    lane = lax.broadcasted_iota(jnp.int32, (rows_x, 128), 1)

    def ahead_z(v):
        return jnp.where(lane < 127, pltpu.roll(v, 127, 1), 0.0)

    def behind_z(v):
        return jnp.where(lane > 0, pltpu.roll(v, 1, 1), 0.0)

    def over_rows(body, stop=rows_y, start=0):
        group = math.gcd(4, stop - start)

        def step(i, carry):
            for k in range(group):
                body(start + i * group + k)
            return carry

        lax.fori_loop(0, (stop - start) // group, step, 0)

    zeros_slab = jnp.zeros((rows_x, 128), jnp.float32)
    zeros_edge = jnp.zeros((EDGE, 128), jnp.float32)
    for s in range(STEPS):
        for c in range(3):
            efield[s, c, own(rows_y), :] = zeros_slab

            def clear(y, s=s, c=c):
                efield[s, c, edge(y, EDGE + rows_x), :] = zeros_edge

            over_rows(clear)

    def native(ref, y):
        return ref[pl.ds(y, rows_x, stride=rows_y), :]

    loads[0].wait()
    for load in loads[2:]:
        load.start()

    def stage(y):
        for c in range(3):
            efield[0, c, own(y), :] = native(v_electric.at[ORDER[c]], y)

    over_rows(stage)
    loads[1].wait()

    distances = sorted({a * a + b * b for a in range(RMAX) for b in range(RMAX) if a * a + b * b < RMAX * RMAX})

    def filtered_sum(ref, emit):
        def pair(y):
            for a in range(1, RMAX):
                sums[a - 1, y] = (
                    ref[rows(y, EDGE + a), :] + ref[rows(y, EDGE - a), :]
                )

        over_rows(pair, rows_y + 2 * WIDTH)

        def gather(y):
            def column(a, b):
                if a == 0:
                    return ref[own(y + WIDTH + b), :]
                return sums[a - 1, y + WIDTH + b]

            by_distance = {}
            for a in range(RMAX):
                for b in range(RMAX):
                    d = a * a + b * b
                    if d not in distances:
                        continue
                    term = column(a, 0) if b == 0 else column(a, b) + column(a, -b)
                    by_distance[d] = by_distance[d] + term if d in by_distance else term
            radius = weight_radius[y]
            total = radius * by_distance[0]
            for d in distances[1:]:
                total = total + jnp.maximum(radius - math.sqrt(d), 0.0) * by_distance[d]
            emit(y, total)

        over_rows(gather)

    def settle():
        for s in range(STEPS):
            for refs, shape, side in (
                (ye_recv, zeros_slab, (0, 1)),
                (yh_recv, zeros_slab, (0, -1)),
                (xe_recv, zeros_edge, (1, 0)),
                (xh_recv, zeros_edge, (-1, 0)),
            ):

                @pl.when(jnp.logical_not(has[side]))
                def _():
                    for k in range(2):
                        refs[s, k] = shape

            for ref, side in ((d1_recv, (1, -1)), (d2_recv, (-1, 1))):

                @pl.when(jnp.logical_not(has[side]))
                def _():
                    ref[s] = zeros_edge

        def frame(ref, i, j):
            xs = {-1: (0, EDGE), 0: (EDGE, rows_x), 1: (EDGE + rows_x, EDGE)}[i]
            ys = {-1: range(WIDTH), 0: range(WIDTH, WIDTH + rows_y), 1: range(WIDTH + rows_y, 2 * WIDTH + rows_y)}[j]
            return xs, ys

        ones_slab = jnp.ones((rows_x, 128), jnp.float32)
        over_rows(lambda y: covered.__setitem__((own(y + WIDTH), slice(None)), ones_slab))
        for i, j in SIDES:
            xs, ys = frame(covered, i, j)
            inside = jnp.where(has[i, j], jnp.float32(1.0), jnp.float32(0.0))
            filler = jnp.zeros((xs[1], 128), jnp.float32) + inside
            for y in ys:
                covered[rows(y, *xs), :] = filler

        for k in range(2):
            for refs, side in ((xf_recv.at[k], (2 * k - 1, 0)), (yf_recv.at[k], (0, 2 * k - 1))):

                @pl.when(jnp.logical_not(has[side]))
                def _():
                    refs[...] = jnp.zeros(refs.shape, jnp.float32)

            for j in range(2):

                @pl.when(jnp.logical_not(has[2 * k - 1, 2 * j - 1]))
                def _():
                    cf_recv[k, j] = jnp.zeros((WIDTH, WIDTH, 128), jnp.float32)

        loads[7].wait()
        radii = v_radius[...].astype(jnp.float32).T
        for y in range(rows_y):
            weight_radius[y] = jnp.broadcast_to(radii[:, y : y + 1], (rows_x, 128))

        filtered_sum(covered, lambda y, total: inv_denom.__setitem__(y, 1.0 / total))

    def column_of(ref, x, first):
        return ref.at[pl.ds(first * slab + EDGE + x, rows_y, stride=slab), :]

    behind_mask_x = jnp.where(has[-1, 0], jnp.float32(COURANT), jnp.float32(0.0))
    behind_mask_y = jnp.where(has[0, -1], jnp.float32(COURANT), jnp.float32(0.0))

    def copies(s):
        base = 6 * s

        def copy(k, src, dst, side):
            return pltpu.make_async_remote_copy(
                src_ref=src,
                dst_ref=dst,
                send_sem=send_sems.at[base + k],
                recv_sem=recv_sems.at[base + k],
                device_id=device(*side),
                device_id_type=MESH,
            )

        return [
            ((0, -1), copy(2, efield.at[s, 0:2, own(0), :], ye_recv.at[s], (0, -1))),
            ((0, 1), copy(3, yh_send.at[s], yh_recv.at[s], (0, 1))),
            ((1, -1), copy(5, efield.at[s, 0, edge(0, rows_x), :], d2_recv.at[s], (1, -1))),
            ((-1, 0), copy(0, xe_send.at[s], xe_recv.at[s], (-1, 0))),
            ((1, 0), copy(1, xh_send.at[s], xh_recv.at[s], (1, 0))),
            ((-1, 1), copy(4, xe_send.at[s, 1], d1_recv.at[s], (-1, 1))),
        ]

    def start(pairs):
        for side, copy in pairs:
            pl.when(has[side])(copy.start)

    def arrive(pairs):
        for (i, j), copy in pairs:
            pl.when(has[-i, -j])(copy.wait_recv)

    def sent(pairs):
        for side, copy in pairs:
            pl.when(has[side])(copy.wait_send)

    def column(y):
        return pl.ds(y * rows_x if isinstance(y, int) else pl.multiple_of(y * rows_x, rows_x), rows_x)

    def curled(s, y):
        ex, ez, ey = (efield[s, c, own(y), :] for c in range(3))
        ex_y, ez_y = (efield[s, c, own(y + 1), :] for c in (0, 1))
        ez_x, ey_x = (efield[s, c, rows(y, EDGE + 1), :] for c in (1, 2))
        if s == 0:
            hx, hz, hy = (native(v_magnetic.at[ORDER[c]], y) for c in range(3))
        else:
            hx, hz, hy = (hfield[s - 1, c, own(y + 1), :] for c in range(3))
        hfield[s, 0, own(y + 1), :] = hx - COURANT * ((ez_y - ez) - (ahead_z(ey) - ey))
        hfield[s, 2, own(y + 1), :] = hy - COURANT * ((ahead_z(ex) - ex) - (ez_x - ez))
        hfield[s, 1, own(y + 1), :] = hz - COURANT * ((ey_x - ey) - (ex_y - ex))

    def driven_by(s, y, fields):
        material = (OMEGA_SQUARED * LORENTZ_STRENGTH) * native(v_density, y)
        scale = inv_eps[y]
        for c in range(3):
            if s == 0:
                p, q = native(v_polar.at[ORDER[c]], y), native(v_rate.at[ORDER[c]], y)
            else:
                p, q = polar[c, y], rate[c, y]
            q = DAMPING * q - OMEGA_SQUARED * p + material * fields[c]
            if s + 1 < STEPS:
                polar[c, y] = p + q
                rate[c, y] = q
            driven[c, y] = fields[c] - q * scale

    def advanced(s, y):
        hx, hz, hy = (hfield[s, c, own(y + 1), :] for c in range(3))
        hx_y, hz_y = (hfield[s, c, own(y), :] for c in (0, 1))
        hz_x, hy_x = (hfield[s, c, rows(y + 1, EDGE - 1), :] for c in (1, 2))
        curls = (
            (hz - hz_y) - (hy - behind_z(hy)),
            (hy - hy_x) - (hx - hx_y),
            (hx - behind_z(hx)) - (hz - hz_x),
        )
        scale = COURANT * inv_eps[y]
        news = [driven[c, y] + curls[c] * scale for c in range(3)]
        total = None
        for c in range(3):
            term = news[c] * native(v_forward.at[3 * s + ORDER[c]], y)
            total = term if total is None else total + term
        return (hx, hz, hy), news, total

    def flip(k, src, dst):
        return pltpu.make_async_remote_copy(
            src_ref=src,
            dst_ref=dst,
            send_sem=send_sems.at[k],
            recv_sem=recv_sems.at[k],
            device_id=mirror,
            device_id_type=MESH,
        )

    def inner_rows():
        def first(y):
            _, news, total = advanced(0, y)
            for c in range(3):
                efield[1, c, own(y), :] = news[c]
            gradient[column(y), :] = total

        over_rows(first, rows_y - 1, 1)
        over_rows(lambda y: curled(1, y), rows_y - 2, 1)

        def second(y):
            material = (OMEGA_SQUARED * LORENTZ_STRENGTH) * native(v_density, y)
            for c in range(3):
                kept[c, y] = driven[c, y]
                e = efield[1, c, own(y), :]
                q = DAMPING * rate[c, y] - OMEGA_SQUARED * polar[c, y] + material * e
                driven[c, y] = e - q * inv_eps[y]
            _, _, total = advanced(1, y)
            g_send[column(y), :] = gradient[column(y), :] + total
            for c in range(3):
                driven[c, y] = kept[c, y]

        over_rows(second, rows_y - 2, 2)

    inner = pl.ds(2 * rows_x, (rows_y - 4) * rows_x)
    flips = [flip(12, g_send.at[inner, :], g_recv.at[inner, :])]
    flips += [flip(13 + k, g_near.at[column(y), :], g_recv.at[column(y), :]) for k, y in enumerate((1, rows_y - 2))]
    flips += [flip(15 + k, gradient.at[column(y), :], g_recv.at[column(y), :]) for k, y in enumerate((0, rows_y - 1))]
    flips += [flip(17 + 9 * k, ends_send.at[pl.ds(2 * (1 - k), 2)], ends_recv.at[pl.ds(2 * (1 - k), 2)]) for k in range(2)]
    ends = (1, rows_x - 2, 0, rows_x - 1)

    def whole(s, y):
        hs, news, total = advanced(s, y)
        for c in range(3):
            if s + 1 < STEPS:
                efield[s + 1, c, own(y), :] = news[c]
            else:
                o_electric[ORDER[c], pl.ds(y, rows_x, stride=rows_y), :] = news[c]
                o_magnetic[ORDER[c], pl.ds(y, rows_x, stride=rows_y), :] = hs[c]
        if s > 0:
            total = gradient[column(y), :] + total
        gradient[column(y), :] = total

    def faces_y(s):
        for k in range(2):
            yh_send[s, k] = hfield[s, k, own(rows_y), :]

    def faces_x(s):
        for k in range(2):
            xe_send[s, k] = column_of(efield.at[s, 1 + k], 0, 0)[...]
            xh_send[s, k] = column_of(hfield.at[s, 1 + k], rows_x - 1, 1)[...]

    def drive(s, y):
        driven_by(s, y, [efield[s, c, own(y), :] for c in range(3)])

    def prepare():
        for load in loads[2:7] + loads[8:]:
            load.wait()
        over_rows(
            lambda y: inv_eps.__setitem__(y, 1.0 / (1.0 + (EPS_MATERIAL - 1.0) * native(v_density, y)))
        )
        over_rows(lambda y: drive(0, y))
        inner_rows()

    pending = []
    for s in range(STEPS):

        pairs = copies(s)
        if s == 0:
            over_rows(lambda y: curled(0, y))
            faces_y(s)
            faces_x(s)
            pl.semaphore_wait(barrier, greeted)
            start(pairs)
        else:
            curled(s, rows_y - 1)
            faces_y(s)
            start(pairs[:3])
            over_rows(lambda y, s=s: whole(s - 1, y), rows_y - 1, 1)
            over_rows(lambda y, s=s: curled(s, y), rows_y - 1)
            faces_x(s)
            start(pairs[3:])
        if s == 0:
            prepare()
            flips[0].start()
            settle()
        else:
            over_rows(lambda y, s=s: drive(s, y))

            def near(y):
                g_near[column(y), :] = gradient[column(y), :] + advanced(STEPS - 1, y)[2]

            over_rows(near, rows_y - 1, 1)
            for k, x in enumerate((1, rows_x - 2)):
                ends_send[k] = g_near[pl.ds(x, rows_y, stride=rows_x), :]
            for copy in flips[1:3] + flips[6:]:
                copy.start()
        arrive(pairs)
        pending += pairs

        hfield[s, 0, own(rows_y), :] = hfield[s, 0, own(rows_y), :] - COURANT * ye_recv[s, 1]
        hfield[s, 1, own(rows_y), :] = hfield[s, 1, own(rows_y), :] + COURANT * ye_recv[s, 0]
        last_z = column_of(hfield.at[s, 1], rows_x - 1, 1)
        last_y = column_of(hfield.at[s, 2], rows_x - 1, 1)
        last_z[...] = last_z[...] - COURANT * xe_recv[s, 1]
        last_y[...] = last_y[...] + COURANT * xe_recv[s, 0]
        hfield[s, 0, own(0), :] = yh_recv[s, 0] - behind_mask_y * efield[s, 1, own(0), :]
        hfield[s, 1, own(0), :] = yh_recv[s, 1] + behind_mask_y * efield[s, 0, own(0), :]
        corner = hfield[s, 1, rows(0, EDGE + rows_x - 1, 1), :]
        hfield[s, 1, rows(0, EDGE + rows_x - 1, 1), :] = corner - COURANT * d1_recv[s, rows_y - 1 : rows_y, :]
        row = lax.broadcasted_iota(jnp.int32, (rows_y, 128), 0)
        extra = jnp.where(row == rows_y - 1, d2_recv[s, EDGE - 1 : EDGE, :], 0.0)
        column_of(hfield.at[s, 1], -1, 1)[...] = xh_recv[s, 0] - behind_mask_x * xe_send[s, 1] + COURANT * extra
        column_of(hfield.at[s, 2], -1, 1)[...] = xh_recv[s, 1] + behind_mask_x * xe_send[s, 0]

        over_rows(lambda k, s=s: whole(s, k * (rows_y - 1)), 2)

    for copy in flips[3:5]:
        copy.start()
    over_rows(lambda y: whole(STEPS - 1, y), rows_y - 1, 1)
    for k, x in enumerate((0, rows_x - 1)):
        ends_send[2 + k] = gradient[pl.ds(x, rows_y, stride=rows_x), :]
    flips[5].start()
    for copy in flips:
        copy.wait_recv()

    def spread(ref, y):
        g_turn[pl.ds(y, rows_x, stride=rows_y), :] = ref[column(y), :]

    over_rows(lambda y: spread(g_recv, y))
    for k, x in enumerate(ends):
        g_turn[pl.ds(x * rows_y, rows_y), :] = ends_recv[k]
    for y in (0, rows_y - 1):
        spread(g_recv, y)

    def turn(x):
        g_flip[pl.ds(pl.multiple_of(x * rows_y, rows_y), rows_y), :] = g_turn[
            pl.ds(pl.multiple_of((rows_x - 1 - x) * rows_y, rows_y), rows_y), :
        ]

    over_rows(turn, rows_x)

    def update(y):
        mirrored = g_flip[pl.ds(partner[y], rows_x, stride=rows_y), :]
        symmetric = 0.5 * (gradient[column(y), :] + mirrored)
        design = native(v_mask, y).astype(jnp.float32)
        updated[own(y + WIDTH), :] = native(v_density, y) - UPDATE_STEP * design * symmetric

    over_rows(update)

    for r in range(WIDTH):
        xf_send[0, r] = column_of(updated, r, WIDTH)[...]
        xf_send[1, r] = column_of(updated, rows_x - WIDTH + r, WIDTH)[...]
        yf_send[0, r] = updated[own(WIDTH + r), :]
        yf_send[1, r] = updated[own(rows_y + r), :]

    halos = []
    for k, (i, j) in enumerate(SIDES):
        if j == 0:
            src, dst = xf_send.at[(i + 1) // 2], xf_recv.at[(1 - i) // 2]
        elif i == 0:
            src, dst = yf_send.at[(j + 1) // 2], yf_recv.at[(1 - j) // 2]
        else:
            xs = slice(0, WIDTH) if i < 0 else slice(rows_x - WIDTH, rows_x)
            src, dst = yf_send.at[(j + 1) // 2, :, xs, :], cf_recv.at[(1 - i) // 2, (1 - j) // 2]
        halos.append(
            (
                (i, j),
                pltpu.make_async_remote_copy(
                    src_ref=src,
                    dst_ref=dst,
                    send_sem=send_sems.at[18 + k],
                    recv_sem=recv_sems.at[18 + k],
                    device_id=device(i, j),
                    device_id_type=MESH,
                ),
            )
        )
    start(halos)
    arrive(halos)
    for r in range(WIDTH):
        column_of(updated, r - WIDTH, WIDTH)[...] = xf_recv[0, r]
        column_of(updated, rows_x + r, WIDTH)[...] = xf_recv[1, r]
        for j in range(2):
            y = r + j * (WIDTH + rows_y)
            updated[own(y), :] = yf_recv[j, r]
            updated[rows(y, EDGE - WIDTH, WIDTH), :] = cf_recv[0, j, r]
            updated[rows(y, EDGE + rows_x, WIDTH), :] = cf_recv[1, j, r]

    top = math.tanh(SHARPNESS * THRESHOLD)
    bottom = top + math.tanh(SHARPNESS * (1.0 - THRESHOLD))

    def project(y, total):
        filtered = total * inv_denom[y]
        o_density[pl.ds(y, rows_x, stride=rows_y), :] = (
            top + jnp.tanh(SHARPNESS * (filtered - THRESHOLD))
        ) / bottom

    filtered_sum(updated, project)
    sent(pending)
    for copy in flips:
        copy.wait_send()
    sent(halos)


def write_out(electric, magnetic, density, electric_out, magnetic_out, density_out, sems):
    pairs = ((electric, electric_out), (magnetic, magnetic_out), (density, density_out))
    pairs = [(src.at[c], dst.at[c]) for src, dst in pairs[:2] for c in range(3)] + [pairs[2]]
    stores = [pltpu.make_async_copy(src, dst, sems.at[k]) for k, (src, dst) in enumerate(pairs)]
    for store in stores:
        store.start()
    for store in stores:
        store.wait()


def local(nx, ny, *args):
    rows_x, rows_y, depth = args[4].shape
    cells = rows_x * rows_y
    slab = rows_x + 2 * EDGE
    f32 = jnp.float32

    def vmem(*shape, dtype=f32):
        return pltpu.VMEM(shape, dtype)

    any_spec = pl.BlockSpec(memory_space=pl.ANY)
    electric, magnetic, polar, rate, density, forward, mask, partners, radius = args
    operands = (
        electric.reshape(3, cells, depth),
        magnetic.reshape(3, cells, depth),
        polar.reshape(3, cells, depth),
        rate.reshape(3, cells, depth),
        density.reshape(cells, depth),
        forward.reshape(3 * STEPS, cells, depth),
        mask.reshape(cells, depth),
        partners,
        radius.T,
    )
    in_specs = [any_spec] * 9
    shapes = ((3, cells, depth), (3, cells, depth), (cells, depth))
    vmem_spec = pl.BlockSpec(memory_space=pltpu.VMEM)
    held = pl.pallas_call(
        functools.partial(kernel, nx, ny),
        out_shape=tuple(pltpu.VMEM(shape, f32) for shape in shapes),
        in_specs=in_specs,
        out_specs=(vmem_spec,) * 3,
        scratch_shapes=[
            vmem(3, cells, depth),
            vmem(3, cells, depth),
            vmem(3, cells, depth),
            vmem(3, cells, depth),
            vmem(cells, depth),
            vmem(3 * STEPS, cells, depth),
            vmem(cells, depth, dtype=jnp.int32),
            vmem(rows_y, rows_x, dtype=jnp.int32),
            pltpu.SMEM((rows_y,), jnp.int32),
            vmem(STEPS, 3, (rows_y + 1) * slab, depth),
            vmem(STEPS, 3, (rows_y + 1) * slab, depth),
            vmem(3, rows_y, rows_x, depth),
            vmem(3, rows_y, rows_x, depth),
            vmem(3, rows_y, rows_x, depth),
            vmem(3, rows_y, rows_x, depth),
            vmem(rows_y, rows_x, depth),
            vmem(cells, depth),
            vmem(cells, depth),
            vmem(cells, depth),
            vmem(cells, depth),
            vmem(cells, depth),
            vmem(cells, depth),
            vmem(4, rows_y, depth),
            vmem(4, rows_y, depth),
            vmem((rows_y + 2 * WIDTH) * slab, depth),
            vmem((rows_y + 2 * WIDTH) * slab, depth),
            vmem(WIDTH, rows_y + 2 * WIDTH, rows_x, depth),
            vmem(rows_y, rows_x, depth),
            vmem(rows_y, rows_x, depth),
            vmem(STEPS, 2, rows_x, depth),
            vmem(STEPS, 2, rows_x, depth),
            vmem(STEPS, 2, rows_x, depth),
            vmem(STEPS, 2, rows_y, depth),
            vmem(STEPS, 2, rows_y, depth),
            vmem(STEPS, 2, rows_y, depth),
            vmem(STEPS, 2, rows_y, depth),
            vmem(STEPS, EDGE, depth),
            vmem(STEPS, EDGE, depth),
            vmem(2, WIDTH, rows_y, depth),
            vmem(2, WIDTH, rows_y, depth),
            vmem(2, WIDTH, rows_x, depth),
            vmem(2, WIDTH, rows_x, depth),
            vmem(2, 2, WIDTH, WIDTH, depth),
            pltpu.SemaphoreType.DMA((9,)),
            pltpu.SemaphoreType.DMA((27,)),
            pltpu.SemaphoreType.DMA((27,)),
        ],
        compiler_params=pltpu.CompilerParams(collective_id=0, has_side_effects=True),
    )(*operands)
    outs = pl.pallas_call(
        write_out,
        out_shape=tuple(jax.ShapeDtypeStruct(shape, f32) for shape in shapes),
        in_specs=[vmem_spec] * 3,
        out_specs=(any_spec,) * 3,
        scratch_shapes=[pltpu.SemaphoreType.DMA((7,))],
    )(*[pltpu.with_memory_space_constraint(a, pltpu.VMEM) for a in held])
    return (
        outs[0].reshape(electric.shape),
        outs[1].reshape(magnetic.shape),
        outs[2].reshape(density.shape),
    )


def solution(mesh):
    in_specs = (
        P(None, "gx", "gy", None),
        P(None, "gx", "gy", None),
        P(None, "gx", "gy", None),
        P(None, "gx", "gy", None),
        P("gx", "gy", None),
        P(None, None, "gx", "gy", None),
        P("gx", "gy", None),
        P("gy"),
        P("gx", "gy"),
    )
    out_specs = (P(None, "gx", "gy", None), P(None, "gx", "gy", None), P("gx", "gy", None))
    return jax.shard_map(
        functools.partial(local, mesh.shape["gx"], mesh.shape["gy"]),
        mesh=mesh,
        in_specs=in_specs,
        out_specs=out_specs,
        check_vma=False,
    )
```

```python
import functools
import math

import jax
import jax.numpy as jnp
from jax import lax
from jax.experimental import pallas as pl
from jax.experimental.pallas import tpu as pltpu
from jax.sharding import PartitionSpec as P

STEPS = 2
RMAX = 4
COURANT = 0.5
DAMPING = 0.9
OMEGA_SQUARED = 0.3
LORENTZ_STRENGTH = 2.0
EPS_MATERIAL = 4.0
UPDATE_STEP = 0.25
SHARPNESS = 4.0
THRESHOLD = 0.5

MESH = pl.DeviceIdType.MESH
WIDTH = RMAX - 1
EDGE = 8
ORDER = (0, 2, 1)
SIDES = tuple((i, j) for i in (-1, 0, 1) for j in (-1, 0, 1) if (i, j) != (0, 0))


def kernel(
    nx,
    ny,
    electric_in,
    magnetic_in,
    polar_in,
    rate_in,
    density_in,
    forward_in,
    mask_in,
    partner_in,
    radius_in,
    o_electric,
    o_magnetic,
    o_density,
    v_electric,
    v_magnetic,
    v_polar,
    v_rate,
    v_density,
    v_forward,
    v_mask,
    v_radius,
    partner,
    efield,
    hfield,
    polar,
    rate,
    driven,
    kept,
    inv_eps,
    gradient,
    g_send,
    g_recv,
    g_turn,
    g_near,
    g_flip,
    ends_send,
    ends_recv,
    updated,
    covered,
    sums,
    weight_radius,
    inv_denom,
    ye_recv,
    yh_send,
    yh_recv,
    xe_send,
    xe_recv,
    xh_send,
    xh_recv,
    d1_recv,
    d2_recv,
    xf_send,
    xf_recv,
    yf_send,
    yf_recv,
    cf_recv,
    in_sems,
    send_sems,
    recv_sems,
):
    rows_y, rows_x = v_radius.shape
    slab = rows_x + 2 * EDGE

    def rows(y, first=EDGE, count=rows_x):
        return pl.ds(y * slab + first, count)

    def own(y):
        start = y * slab + EDGE
        return pl.ds(start if isinstance(start, int) else pl.multiple_of(start, EDGE), rows_x)

    def edge(y, first):
        start = y * slab + first
        return pl.ds(start if isinstance(start, int) else pl.multiple_of(start, EDGE), EDGE)

    gx, gy = lax.axis_index("gx"), lax.axis_index("gy")
    has = {}
    for i, j in SIDES:
        parts = []
        if i:
            parts.append(gx > 0 if i < 0 else gx < nx - 1)
        if j:
            parts.append(gy > 0 if j < 0 else gy < ny - 1)
        has[i, j] = functools.reduce(jnp.logical_and, parts)

    def device(i, j):
        return (lax.rem(gx + i + nx, nx), lax.rem(gy + j + ny, ny))

    mirror = (nx - 1 - gx, gy)

    barrier = pltpu.get_barrier_semaphore()
    pl.semaphore_signal(barrier, inc=1, device_id=mirror, device_id_type=MESH)
    greeted = jnp.int32(1)
    for side in sorted(SIDES, key=lambda p: (abs(p[0]), -abs(p[1]))):
        greeted = greeted + has[side].astype(jnp.int32)

        @pl.when(has[side])
        def _():
            pl.semaphore_signal(barrier, inc=1, device_id=device(*side), device_id_type=MESH)


    loads = [
        pltpu.make_async_copy(src, dst, in_sems.at[k])
        for k, (src, dst) in enumerate(
            [
                (electric_in, v_electric),
                (magnetic_in, v_magnetic),
                (polar_in, v_polar),
                (rate_in, v_rate),
                (density_in, v_density),
                (forward_in, v_forward),
                (mask_in, v_mask),
                (radius_in, v_radius),
                (partner_in, partner),
            ]
        )
    ]
    loads[0].start()
    loads[1].start()

    lane = lax.broadcasted_iota(jnp.int32, (rows_x, 128), 1)

    def ahead_z(v):
        return jnp.where(lane < 127, pltpu.roll(v, 127, 1), 0.0)

    def behind_z(v):
        return jnp.where(lane > 0, pltpu.roll(v, 1, 1), 0.0)

    def over_rows(body, stop=rows_y, start=0):
        group = math.gcd(4, stop - start)

        def step(i, carry):
            for k in range(group):
                body(start + i * group + k)
            return carry

        lax.fori_loop(0, (stop - start) // group, step, 0)

    zeros_slab = jnp.zeros((rows_x, 128), jnp.float32)
    zeros_edge = jnp.zeros((EDGE, 128), jnp.float32)
    for s in range(STEPS):
        for c in range(3):
            efield[s, c, own(rows_y), :] = zeros_slab

            def clear(y, s=s, c=c):
                efield[s, c, edge(y, EDGE + rows_x), :] = zeros_edge

            over_rows(clear)

    def native(ref, y):
        return ref[pl.ds(y, rows_x, stride=rows_y), :]

    loads[0].wait()
    for load in loads[2:]:
        load.start()

    def stage(y):
        for c in range(3):
            efield[0, c, own(y), :] = native(v_electric.at[ORDER[c]], y)

    over_rows(stage)
    loads[1].wait()

    distances = sorted({a * a + b * b for a in range(RMAX) for b in range(RMAX) if a * a + b * b < RMAX * RMAX})

    def filtered_sum(ref, emit):
        def pair(y):
            for a in range(1, RMAX):
                sums[a - 1, y] = (
                    ref[rows(y, EDGE + a), :] + ref[rows(y, EDGE - a), :]
                )

        over_rows(pair, rows_y + 2 * WIDTH)

        def gather(y):
            def column(a, b):
                if a == 0:
                    return ref[own(y + WIDTH + b), :]
                return sums[a - 1, y + WIDTH + b]

            by_distance = {}
            for a in range(RMAX):
                for b in range(RMAX):
                    d = a * a + b * b
                    if d not in distances:
                        continue
                    term = column(a, 0) if b == 0 else column(a, b) + column(a, -b)
                    by_distance[d] = by_distance[d] + term if d in by_distance else term
            radius = weight_radius[y]
            total = radius * by_distance[0]
            for d in distances[1:]:
                total = total + jnp.maximum(radius - math.sqrt(d), 0.0) * by_distance[d]
            emit(y, total)

        over_rows(gather)

    def settle():
        for s in range(STEPS):
            for refs, shape, side in (
                (ye_recv, zeros_slab, (0, 1)),
                (yh_recv, zeros_slab, (0, -1)),
                (xe_recv, zeros_edge, (1, 0)),
                (xh_recv, zeros_edge, (-1, 0)),
            ):

                @pl.when(jnp.logical_not(has[side]))
                def _():
                    for k in range(2):
                        refs[s, k] = shape

            for ref, side in ((d1_recv, (1, -1)), (d2_recv, (-1, 1))):

                @pl.when(jnp.logical_not(has[side]))
                def _():
                    ref[s] = zeros_edge

        def frame(ref, i, j):
            xs = {-1: (0, EDGE), 0: (EDGE, rows_x), 1: (EDGE + rows_x, EDGE)}[i]
            ys = {-1: range(WIDTH), 0: range(WIDTH, WIDTH + rows_y), 1: range(WIDTH + rows_y, 2 * WIDTH + rows_y)}[j]
            return xs, ys

        ones_slab = jnp.ones((rows_x, 128), jnp.float32)
        over_rows(lambda y: covered.__setitem__((own(y + WIDTH), slice(None)), ones_slab))
        for i, j in SIDES:
            xs, ys = frame(covered, i, j)
            inside = jnp.where(has[i, j], jnp.float32(1.0), jnp.float32(0.0))
            filler = jnp.zeros((xs[1], 128), jnp.float32) + inside
            for y in ys:
                covered[rows(y, *xs), :] = filler

        for k in range(2):
            for refs, side in ((xf_recv.at[k], (2 * k - 1, 0)), (yf_recv.at[k], (0, 2 * k - 1))):

                @pl.when(jnp.logical_not(has[side]))
                def _():
                    refs[...] = jnp.zeros(refs.shape, jnp.float32)

            for j in range(2):

                @pl.when(jnp.logical_not(has[2 * k - 1, 2 * j - 1]))
                def _():
                    cf_recv[k, j] = jnp.zeros((WIDTH, WIDTH, 128), jnp.float32)

        loads[7].wait()
        radii = v_radius[...].astype(jnp.float32).T
        for y in range(rows_y):
            weight_radius[y] = jnp.broadcast_to(radii[:, y : y + 1], (rows_x, 128))

        filtered_sum(covered, lambda y, total: inv_denom.__setitem__(y, 1.0 / total))

    def column_of(ref, x, first):
        return ref.at[pl.ds(first * slab + EDGE + x, rows_y, stride=slab), :]

    behind_mask_x = jnp.where(has[-1, 0], jnp.float32(COURANT), jnp.float32(0.0))
    behind_mask_y = jnp.where(has[0, -1], jnp.float32(COURANT), jnp.float32(0.0))

    def copies(s):
        base = 6 * s

        def copy(k, src, dst, side):
            return pltpu.make_async_remote_copy(
                src_ref=src,
                dst_ref=dst,
                send_sem=send_sems.at[base + k],
                recv_sem=recv_sems.at[base + k],
                device_id=device(*side),
                device_id_type=MESH,
            )

        return [
            ((0, -1), copy(2, efield.at[s, 0:2, own(0), :], ye_recv.at[s], (0, -1))),
            ((0, 1), copy(3, yh_send.at[s], yh_recv.at[s], (0, 1))),
            ((1, -1), copy(5, efield.at[s, 0, edge(0, rows_x), :], d2_recv.at[s], (1, -1))),
            ((-1, 0), copy(0, xe_send.at[s], xe_recv.at[s], (-1, 0))),
            ((1, 0), copy(1, xh_send.at[s], xh_recv.at[s], (1, 0))),
            ((-1, 1), copy(4, xe_send.at[s, 1], d1_recv.at[s], (-1, 1))),
        ]

    def start(pairs):
        for side, copy in pairs:
            pl.when(has[side])(copy.start)

    def arrive(pairs):
        for (i, j), copy in pairs:
            pl.when(has[-i, -j])(copy.wait_recv)

    def sent(pairs):
        for side, copy in pairs:
            pl.when(has[side])(copy.wait_send)

    def column(y):
        return pl.ds(y * rows_x if isinstance(y, int) else pl.multiple_of(y * rows_x, rows_x), rows_x)

    def curled(s, y):
        ex, ez, ey = (efield[s, c, own(y), :] for c in range(3))
        ex_y, ez_y = (efield[s, c, own(y + 1), :] for c in (0, 1))
        ez_x, ey_x = (efield[s, c, rows(y, EDGE + 1), :] for c in (1, 2))
        if s == 0:
            hx, hz, hy = (native(v_magnetic.at[ORDER[c]], y) for c in range(3))
        else:
            hx, hz, hy = (hfield[s - 1, c, own(y + 1), :] for c in range(3))
        hfield[s, 0, own(y + 1), :] = hx - COURANT * ((ez_y - ez) - (ahead_z(ey) - ey))
        hfield[s, 2, own(y + 1), :] = hy - COURANT * ((ahead_z(ex) - ex) - (ez_x - ez))
        hfield[s, 1, own(y + 1), :] = hz - COURANT * ((ey_x - ey) - (ex_y - ex))

    def driven_by(s, y, fields):
        material = (OMEGA_SQUARED * LORENTZ_STRENGTH) * native(v_density, y)
        scale = inv_eps[y]
        for c in range(3):
            if s == 0:
                p, q = native(v_polar.at[ORDER[c]], y), native(v_rate.at[ORDER[c]], y)
            else:
                p, q = polar[c, y], rate[c, y]
            q = DAMPING * q - OMEGA_SQUARED * p + material * fields[c]
            if s + 1 < STEPS:
                polar[c, y] = p + q
                rate[c, y] = q
            driven[c, y] = fields[c] - q * scale

    def advanced(s, y):
        hx, hz, hy = (hfield[s, c, own(y + 1), :] for c in range(3))
        hx_y, hz_y = (hfield[s, c, own(y), :] for c in (0, 1))
        hz_x, hy_x = (hfield[s, c, rows(y + 1, EDGE - 1), :] for c in (1, 2))
        curls = (
            (hz - hz_y) - (hy - behind_z(hy)),
            (hy - hy_x) - (hx - hx_y),
            (hx - behind_z(hx)) - (hz - hz_x),
        )
        scale = COURANT * inv_eps[y]
        news = [driven[c, y] + curls[c] * scale for c in range(3)]
        total = None
        for c in range(3):
            term = news[c] * native(v_forward.at[3 * s + ORDER[c]], y)
            total = term if total is None else total + term
        return (hx, hz, hy), news, total

    def flip(k, src, dst):
        return pltpu.make_async_remote_copy(
            src_ref=src,
            dst_ref=dst,
            send_sem=send_sems.at[k],
            recv_sem=recv_sems.at[k],
            device_id=mirror,
            device_id_type=MESH,
        )

    def inner_rows():
        def first(y):
            _, news, total = advanced(0, y)
            for c in range(3):
                efield[1, c, own(y), :] = news[c]
            gradient[column(y), :] = total

        over_rows(first, rows_y - 1, 1)
        over_rows(lambda y: curled(1, y), rows_y - 2, 1)

        def second(y):
            material = (OMEGA_SQUARED * LORENTZ_STRENGTH) * native(v_density, y)
            for c in range(3):
                kept[c, y] = driven[c, y]
                e = efield[1, c, own(y), :]
                q = DAMPING * rate[c, y] - OMEGA_SQUARED * polar[c, y] + material * e
                driven[c, y] = e - q * inv_eps[y]
            _, _, total = advanced(1, y)
            g_send[column(y), :] = gradient[column(y), :] + total
            for c in range(3):
                driven[c, y] = kept[c, y]

        over_rows(second, rows_y - 2, 2)

    inner = pl.ds(2 * rows_x, (rows_y - 4) * rows_x)
    flips = [flip(12, g_send.at[inner, :], g_recv.at[inner, :])]
    flips += [flip(13 + k, g_near.at[column(y), :], g_recv.at[column(y), :]) for k, y in enumerate((1, rows_y - 2))]
    flips += [flip(15 + k, gradient.at[column(y), :], g_recv.at[column(y), :]) for k, y in enumerate((0, rows_y - 1))]
    flips += [flip(17 + 9 * k, ends_send.at[pl.ds(2 * (1 - k), 2)], ends_recv.at[pl.ds(2 * (1 - k), 2)]) for k in range(2)]
    ends = (1, rows_x - 2, 0, rows_x - 1)

    def whole(s, y):
        hs, news, total = advanced(s, y)
        for c in range(3):
            if s + 1 < STEPS:
                efield[s + 1, c, own(y), :] = news[c]
            else:
                o_electric[ORDER[c], pl.ds(y, rows_x, stride=rows_y), :] = news[c]
                o_magnetic[ORDER[c], pl.ds(y, rows_x, stride=rows_y), :] = hs[c]
        if s > 0:
            total = gradient[column(y), :] + total
        gradient[column(y), :] = total

    def faces_y(s):
        for k in range(2):
            yh_send[s, k] = hfield[s, k, own(rows_y), :]

    def faces_x(s):
        for k in range(2):
            xe_send[s, k] = column_of(efield.at[s, 1 + k], 0, 0)[...]
            xh_send[s, k] = column_of(hfield.at[s, 1 + k], rows_x - 1, 1)[...]

    def drive(s, y):
        driven_by(s, y, [efield[s, c, own(y), :] for c in range(3)])

    def prepare():
        for load in loads[2:7] + loads[8:]:
            load.wait()
        over_rows(
            lambda y: inv_eps.__setitem__(y, 1.0 / (1.0 + (EPS_MATERIAL - 1.0) * native(v_density, y)))
        )
        over_rows(lambda y: drive(0, y))
        inner_rows()

    pending = []
    for s in range(STEPS):

        pairs = copies(s)
        if s == 0:
            over_rows(lambda y: curled(0, y))
            faces_y(s)
            faces_x(s)
            pl.semaphore_wait(barrier, greeted)
            start(pairs)
        else:
            curled(s, rows_y - 1)
            faces_y(s)
            start(pairs[:3])
            over_rows(lambda y, s=s: whole(s - 1, y), rows_y - 1, 1)
            over_rows(lambda y, s=s: curled(s, y), rows_y - 1)
            faces_x(s)
            start(pairs[3:])
        if s == 0:
            prepare()
            flips[0].start()
            settle()
        else:
            over_rows(lambda y, s=s: drive(s, y))

            def near(y):
                g_near[column(y), :] = gradient[column(y), :] + advanced(STEPS - 1, y)[2]

            over_rows(near, rows_y - 1, 1)
            for k, x in enumerate((1, rows_x - 2)):
                ends_send[k] = g_near[pl.ds(x, rows_y, stride=rows_x), :]
            for copy in flips[1:3] + flips[6:]:
                copy.start()
        arrive(pairs)
        pending += pairs

        hfield[s, 0, own(rows_y), :] = hfield[s, 0, own(rows_y), :] - COURANT * ye_recv[s, 1]
        hfield[s, 1, own(rows_y), :] = hfield[s, 1, own(rows_y), :] + COURANT * ye_recv[s, 0]
        last_z = column_of(hfield.at[s, 1], rows_x - 1, 1)
        last_y = column_of(hfield.at[s, 2], rows_x - 1, 1)
        last_z[...] = last_z[...] - COURANT * xe_recv[s, 1]
        last_y[...] = last_y[...] + COURANT * xe_recv[s, 0]
        hfield[s, 0, own(0), :] = yh_recv[s, 0] - behind_mask_y * efield[s, 1, own(0), :]
        hfield[s, 1, own(0), :] = yh_recv[s, 1] + behind_mask_y * efield[s, 0, own(0), :]
        corner = hfield[s, 1, rows(0, EDGE + rows_x - 1, 1), :]
        hfield[s, 1, rows(0, EDGE + rows_x - 1, 1), :] = corner - COURANT * d1_recv[s, rows_y - 1 : rows_y, :]
        row = lax.broadcasted_iota(jnp.int32, (rows_y, 128), 0)
        extra = jnp.where(row == rows_y - 1, d2_recv[s, EDGE - 1 : EDGE, :], 0.0)
        column_of(hfield.at[s, 1], -1, 1)[...] = xh_recv[s, 0] - behind_mask_x * xe_send[s, 1] + COURANT * extra
        column_of(hfield.at[s, 2], -1, 1)[...] = xh_recv[s, 1] + behind_mask_x * xe_send[s, 0]

        over_rows(lambda k, s=s: whole(s, k * (rows_y - 1)), 2)

    for copy in flips[3:5]:
        copy.start()
    over_rows(lambda y: whole(STEPS - 1, y), rows_y - 1, 1)
    for k, x in enumerate((0, rows_x - 1)):
        ends_send[2 + k] = gradient[pl.ds(x, rows_y, stride=rows_x), :]
    flips[5].start()
    def weigh(y):
        step = (0.5 * UPDATE_STEP) * native(v_mask, y).astype(jnp.float32)
        kept[0, y] = native(v_density, y) - step * gradient[column(y), :]
        kept[1, y] = step

    over_rows(weigh)

    def spread(y):
        g_turn[pl.ds(y, rows_x, stride=rows_y), :] = g_recv[column(y), :]

    for copy in flips[:3] + flips[6:]:
        copy.wait_recv()
    over_rows(spread, rows_y - 1, 1)
    for k in (0, 1):
        g_turn[pl.ds(ends[k] * rows_y, rows_y), :] = ends_recv[k]
    for copy in flips[3:6]:
        copy.wait_recv()
    for k in (2, 3):
        g_turn[pl.ds(ends[k] * rows_y, rows_y), :] = ends_recv[k]
    for y in (0, rows_y - 1):
        spread(y)

    def turn(x):
        g_flip[pl.ds(pl.multiple_of(x * rows_y, rows_y), rows_y), :] = g_turn[
            pl.ds(pl.multiple_of((rows_x - 1 - x) * rows_y, rows_y), rows_y), :
        ]

    over_rows(turn, rows_x)

    def update(y):
        mirrored = g_flip[pl.ds(partner[y], rows_x, stride=rows_y), :]
        updated[own(y + WIDTH), :] = kept[0, y] - kept[1, y] * mirrored

    over_rows(update)

    for r in range(WIDTH):
        xf_send[0, r] = column_of(updated, r, WIDTH)[...]
        xf_send[1, r] = column_of(updated, rows_x - WIDTH + r, WIDTH)[...]
        yf_send[0, r] = updated[own(WIDTH + r), :]
        yf_send[1, r] = updated[own(rows_y + r), :]

    halos = []
    for k, (i, j) in enumerate(SIDES):
        if j == 0:
            src, dst = xf_send.at[(i + 1) // 2], xf_recv.at[(1 - i) // 2]
        elif i == 0:
            src, dst = yf_send.at[(j + 1) // 2], yf_recv.at[(1 - j) // 2]
        else:
            xs = slice(0, WIDTH) if i < 0 else slice(rows_x - WIDTH, rows_x)
            src, dst = yf_send.at[(j + 1) // 2, :, xs, :], cf_recv.at[(1 - i) // 2, (1 - j) // 2]
        halos.append(
            (
                (i, j),
                pltpu.make_async_remote_copy(
                    src_ref=src,
                    dst_ref=dst,
                    send_sem=send_sems.at[18 + k],
                    recv_sem=recv_sems.at[18 + k],
                    device_id=device(i, j),
                    device_id_type=MESH,
                ),
            )
        )
    start(halos)
    arrive(halos)
    for r in range(WIDTH):
        column_of(updated, r - WIDTH, WIDTH)[...] = xf_recv[0, r]
        column_of(updated, rows_x + r, WIDTH)[...] = xf_recv[1, r]
        for j in range(2):
            y = r + j * (WIDTH + rows_y)
            updated[own(y), :] = yf_recv[j, r]
            updated[rows(y, EDGE - WIDTH, WIDTH), :] = cf_recv[0, j, r]
            updated[rows(y, EDGE + rows_x, WIDTH), :] = cf_recv[1, j, r]

    top = math.tanh(SHARPNESS * THRESHOLD)
    bottom = top + math.tanh(SHARPNESS * (1.0 - THRESHOLD))

    def project(y, total):
        filtered = total * inv_denom[y]
        o_density[pl.ds(y, rows_x, stride=rows_y), :] = (
            top + jnp.tanh(SHARPNESS * (filtered - THRESHOLD))
        ) / bottom

    filtered_sum(updated, project)
    sent(pending)
    for copy in flips:
        copy.wait_send()
    sent(halos)


def write_out(electric, magnetic, density, electric_out, magnetic_out, density_out, sems):
    pairs = ((electric, electric_out), (magnetic, magnetic_out), (density, density_out))
    pairs = [(src.at[c], dst.at[c]) for src, dst in pairs[:2] for c in range(3)] + [pairs[2]]
    stores = [pltpu.make_async_copy(src, dst, sems.at[k]) for k, (src, dst) in enumerate(pairs)]
    for store in stores:
        store.start()
    for store in stores:
        store.wait()


def local(nx, ny, *args):
    rows_x, rows_y, depth = args[4].shape
    cells = rows_x * rows_y
    slab = rows_x + 2 * EDGE
    f32 = jnp.float32

    def vmem(*shape, dtype=f32):
        return pltpu.VMEM(shape, dtype)

    any_spec = pl.BlockSpec(memory_space=pl.ANY)
    electric, magnetic, polar, rate, density, forward, mask, partners, radius = args
    operands = (
        electric.reshape(3, cells, depth),
        magnetic.reshape(3, cells, depth),
        polar.reshape(3, cells, depth),
        rate.reshape(3, cells, depth),
        density.reshape(cells, depth),
        forward.reshape(3 * STEPS, cells, depth),
        mask.reshape(cells, depth),
        partners,
        radius.T,
    )
    in_specs = [any_spec] * 9
    shapes = ((3, cells, depth), (3, cells, depth), (cells, depth))
    vmem_spec = pl.BlockSpec(memory_space=pltpu.VMEM)
    held = pl.pallas_call(
        functools.partial(kernel, nx, ny),
        out_shape=tuple(pltpu.VMEM(shape, f32) for shape in shapes),
        in_specs=in_specs,
        out_specs=(vmem_spec,) * 3,
        scratch_shapes=[
            vmem(3, cells, depth),
            vmem(3, cells, depth),
            vmem(3, cells, depth),
            vmem(3, cells, depth),
            vmem(cells, depth),
            vmem(3 * STEPS, cells, depth),
            vmem(cells, depth, dtype=jnp.int32),
            vmem(rows_y, rows_x, dtype=jnp.int32),
            pltpu.SMEM((rows_y,), jnp.int32),
            vmem(STEPS, 3, (rows_y + 1) * slab, depth),
            vmem(STEPS, 3, (rows_y + 1) * slab, depth),
            vmem(3, rows_y, rows_x, depth),
            vmem(3, rows_y, rows_x, depth),
            vmem(3, rows_y, rows_x, depth),
            vmem(3, rows_y, rows_x, depth),
            vmem(rows_y, rows_x, depth),
            vmem(cells, depth),
            vmem(cells, depth),
            vmem(cells, depth),
            vmem(cells, depth),
            vmem(cells, depth),
            vmem(cells, depth),
            vmem(4, rows_y, depth),
            vmem(4, rows_y, depth),
            vmem((rows_y + 2 * WIDTH) * slab, depth),
            vmem((rows_y + 2 * WIDTH) * slab, depth),
            vmem(WIDTH, rows_y + 2 * WIDTH, rows_x, depth),
            vmem(rows_y, rows_x, depth),
            vmem(rows_y, rows_x, depth),
            vmem(STEPS, 2, rows_x, depth),
            vmem(STEPS, 2, rows_x, depth),
            vmem(STEPS, 2, rows_x, depth),
            vmem(STEPS, 2, rows_y, depth),
            vmem(STEPS, 2, rows_y, depth),
            vmem(STEPS, 2, rows_y, depth),
            vmem(STEPS, 2, rows_y, depth),
            vmem(STEPS, EDGE, depth),
            vmem(STEPS, EDGE, depth),
            vmem(2, WIDTH, rows_y, depth),
            vmem(2, WIDTH, rows_y, depth),
            vmem(2, WIDTH, rows_x, depth),
            vmem(2, WIDTH, rows_x, depth),
            vmem(2, 2, WIDTH, WIDTH, depth),
            pltpu.SemaphoreType.DMA((9,)),
            pltpu.SemaphoreType.DMA((27,)),
            pltpu.SemaphoreType.DMA((27,)),
        ],
        compiler_params=pltpu.CompilerParams(collective_id=0, has_side_effects=True),
    )(*operands)
    outs = pl.pallas_call(
        write_out,
        out_shape=tuple(jax.ShapeDtypeStruct(shape, f32) for shape in shapes),
        in_specs=[vmem_spec] * 3,
        out_specs=(any_spec,) * 3,
        scratch_shapes=[pltpu.SemaphoreType.DMA((7,))],
    )(*[pltpu.with_memory_space_constraint(a, pltpu.VMEM) for a in held])
    return (
        outs[0].reshape(electric.shape),
        outs[1].reshape(magnetic.shape),
        outs[2].reshape(density.shape),
    )


def solution(mesh):
    in_specs = (
        P(None, "gx", "gy", None),
        P(None, "gx", "gy", None),
        P(None, "gx", "gy", None),
        P(None, "gx", "gy", None),
        P("gx", "gy", None),
        P(None, None, "gx", "gy", None),
        P("gx", "gy", None),
        P("gy"),
        P("gx", "gy"),
    )
    out_specs = (P(None, "gx", "gy", None), P(None, "gx", "gy", None), P("gx", "gy", None))
    return jax.shard_map(
        functools.partial(local, mesh.shape["gx"], mesh.shape["gy"]),
        mesh=mesh,
        in_specs=in_specs,
        out_specs=out_specs,
        check_vma=False,
    )
```
